256 devices in a mesh: lat: 8 (over x, core), lon: 32 (over y, z).
Axes of the slice: x: 4, y: 4, z: 8, core: 2. Of those that a mesh axis runs over, the one named last changes fastest.
Arguments:
- velocity: bfloat16 [2, 256, 1536, 1024], P(None, None, 'lon', 'lat'), may hold values from -16 to 16
- lon_metric: float32 [1536, 1024], P('lon', 'lat'), may hold values from 0.5 to 2
- lat_metric: float32 [1536, 1024], P('lon', 'lat'), may hold values from 0.5 to 2
- wet_index: int32 [1572864], P(('lat', 'lon')), may hold values from 0 to 6143, as said below
- wet_count: int32 [256], P(('lat', 'lon')), may hold values from 3072 to 6144, as said below
Outputs:
- basis: bfloat16 [512, 1572864], P(None, ('lat', 'lon'))
- r_factor: float32 [512, 512], replicated
The draws below stay inside these ranges and needn't reach their ends.
Inputs may be any that keep to these rules, and one draw needn't show every extreme that they name: `wet_index`: each device's 6144 entries are a permutation of its local cells 0 to 6143. `wet_count`: some device has all 6144 cells wet.
All inputs are finite; a program needn't handle non-finite values.
Results may differ from the reference program's by a relative error of at most 0.001.
The reference program's roundings to bfloat16 on the way (of `fields` and `snapshot`) count: a program that leaves them out, or rounds other values in their place, can miss the bound.
Values may be sent and summed in bfloat16 or wider, within the bound.
A program may use at most 128 MiB of HBM per device.

```python
import math
import jax
import jax.numpy as jnp
from jax import lax

S = 256
CX = 48
CY = 128
CELLS = 6144
NX = 1536
NY = 1024
ROWS = 1572864
N_LAT = 8
N_LON = 32


def draw_velocity(key, part):
    keyed = jax.random.fold_in(key, 3)
    key_base, key_amp, key_noise = jax.random.split(keyed, 3)
    position = jnp.arange(NY, dtype=jnp.float32) / max(NY - 1, 1)
    base_flow = jax.random.normal(key_base, (2, 1, NX, NY), jnp.float32)
    amplitude = jax.random.uniform(key_amp, (1, S, 1, 1), jnp.float32, 0.5, 1.5)
    anomaly = jax.random.normal(key_noise, (2, S, NX, NY), jnp.float32)
    lat_scale = 1.0 + 2.0 * position
    values = (base_flow * amplitude + anomaly) * lat_scale[None, None, None, :]
    return jnp.clip(values, -16.0, 16.0).astype(jnp.bfloat16)


def wet_plan(key):
    keyed = jax.random.fold_in(key, 7)
    key_count, key_full, key_perm = jax.random.split(keyed, 3)
    devices = ROWS // CELLS
    counts = jax.random.randint(key_count, (devices,), CELLS // 2, CELLS + 1)
    full_device = jax.random.randint(key_full, (), 0, devices)
    counts = jnp.where(jnp.arange(devices) == full_device, CELLS, counts).astype(jnp.int32)
    perm_keys = jax.random.split(key_perm, devices)
    orders = jax.vmap(lambda single: jax.random.permutation(single, CELLS))(perm_keys)
    return (counts, orders.reshape(-1).astype(jnp.int32))


def draw_wet_index(key, part):
    return wet_plan(key)[1]


def draw_wet_count(key, part):
    return wet_plan(key)[0]


def shard_levels(own_key, extent, shards, low, high):
    gain = 1.0
    for axis_at, shards_of in shards:
        draws = jax.random.uniform(jax.random.fold_in(jax.random.fold_in(own_key, 6), axis_at), (shards_of,), jnp.float32, low / len(shards), high / len(shards))
        gain = gain * jnp.repeat(jnp.exp(draws), extent[axis_at] // shards_of).reshape((-1,) + (1,) * (len(extent) - 1 - axis_at))
    return gain


def setup_inputs(seed: int = 0) -> dict:
    key_of = jax.random.split(jax.random.key(seed), 6)
    velocity = draw_velocity(jax.random.fold_in(key_of[5], 71), 0)
    lon_metric = jnp.clip(jnp.exp(math.log(2.0) - 1.3862944 * jax.random.uniform(key_of[1], (NX, NY), jnp.float32) ** shard_levels(key_of[1], (NX, NY), ((0, 32), (1, 8)), -0.2, 0.2)), 0.5, 2.0)
    lat_metric = jnp.clip(jnp.exp(math.log(2.0) - 1.3862944 * jax.random.uniform(key_of[2], (NX, NY), jnp.float32) ** shard_levels(key_of[2], (NX, NY), ((0, 32), (1, 8)), -0.2, 0.2)), 0.5, 2.0)
    wet_index = draw_wet_index(jax.random.fold_in(key_of[5], 71), 0)
    wet_count = draw_wet_count(jax.random.fold_in(key_of[5], 71), 0)
    return dict(velocity=velocity, lon_metric=lon_metric, lat_metric=lat_metric, wet_index=wet_index, wet_count=wet_count)


def one_day(pair, lon_metric, lat_metric):
    vel32 = pair.astype(jnp.float32)
    east_cell = jnp.roll(vel32, -1, axis=1)
    west_cell = jnp.roll(vel32, 1, axis=1)
    ghost_row = -vel32[:, ::-1, -1]
    above = jnp.concatenate([vel32[:, :, 1:], ghost_row[:, :, None]], axis=2)
    below = jnp.concatenate([jnp.zeros_like(vel32[:, :, :1]), vel32[:, :, :-1]], axis=2)
    across = 0.5 * lon_metric * (east_cell - west_cell)
    along = 0.5 * lat_metric * (above - below)
    zeta = across[1] - along[0]
    divergence = across[0] + along[1]
    return jnp.stack([zeta, divergence]).astype(jnp.bfloat16)

def reference(velocity, lon_metric, lat_metric, wet_index, wet_count):
    days = jnp.transpose(velocity, (1, 0, 2, 3))
    daily = lax.map(lambda pair: one_day(pair, lon_metric, lat_metric), days)
    fields = jnp.transpose(daily, (1, 0, 2, 3)).reshape(2 * S, NX, NY)
    devices = N_LAT * N_LON
    blocks = fields.reshape(2 * S, N_LON, CX, N_LAT, CY).transpose(0, 3, 1, 2, 4).reshape(2 * S, devices, CELLS)
    index_table = wet_index.reshape(devices, CELLS).astype(jnp.int32)
    picked = jnp.take_along_axis(blocks, index_table[None, :, :], axis=2)
    live = jnp.arange(CELLS, dtype=jnp.int32)[None, :] < wet_count[:, None]
    picked = jnp.where(live[None, :, :], picked, jnp.zeros_like(picked))
    snapshot = picked.reshape(2 * S, ROWS).T.astype(jnp.float32)
    ortho, triangle = jnp.linalg.qr(snapshot)
    signs = jnp.sign(jnp.diagonal(triangle))
    triangle = signs[:, None] * triangle
    ortho = ortho * signs[None, :]
    scale = math.sqrt(ROWS)
    basis = (ortho.T * scale).astype(jnp.bfloat16)
    return (basis, triangle / scale)
```

```python
import functools
import math

import jax
import jax.numpy as jnp
from jax import lax
from jax.experimental import pallas as pl
from jax.experimental.pallas import tpu as pltpu
from jax.sharding import PartitionSpec as P

MESH = pl.DeviceIdType.MESH
VMEM = pl.BlockSpec(memory_space=pltpu.VMEM)
SMEM = pl.BlockSpec(memory_space=pltpu.SMEM)
ANY = pl.BlockSpec(memory_space=pl.ANY)
BIG = 60 << 20
NT = (((1,), (1,)), ((), ()))
TN = (((0,), (0,)), ((), ()))
NN = (((1,), (0,)), ((), ()))


def metric_kernel(idx_ref, count_ref, lon_ref, lat_ref, lon_out, lat_out):
    count = count_ref[0]
    pieces, width = idx_ref.shape
    nx, ny = lon_ref.shape
    total = jnp.zeros((nx, ny), jnp.float32)
    for at in range(pieces):
        cell = idx_ref[at : at + 1, :]
        place = lax.broadcasted_iota(jnp.int32, (1, width), 1) + at * width
        column = jnp.where(place < count, cell // ny, -1)
        row = cell % ny
        hot_x = (lax.broadcasted_iota(jnp.int32, (nx, width), 0) == column).astype(jnp.float32)
        hot_y = (lax.broadcasted_iota(jnp.int32, (ny, width), 0) == row).astype(jnp.float32)
        total += lax.dot_general(
            hot_x.astype(jnp.bfloat16),
            hot_y.astype(jnp.bfloat16),
            NT,
            preferred_element_type=jnp.float32,
        )
    lon_out[...] = 0.5 * lon_ref[...] * total
    lat_out[...] = 0.5 * lat_ref[...] * total


def turn_kernel(v_ref, o_ref, north_ref, south_ref, scr):
    scr[...] = v_ref[...].astype(jnp.float32)
    for x in range(v_ref.shape[1]):
        turned = scr[:, x, :].T
        o_ref[x] = turned.astype(jnp.bfloat16)
        north_ref[x : x + 1, :] = turned[-1:, :]
        south_ref[x : x + 1, :] = turned[:1, :]


def halo_kernel(n_lat, n_lon, vt, north_edge, south_edge, west, east, south, north, send, recv):
    lat, lon = lax.axis_index("lat"), lax.axis_index("lon")
    last = vt.shape[0] - 1
    right = (lat, lax.rem(lon + 1, n_lon))
    left = (lat, lax.rem(lon + n_lon - 1, n_lon))
    is_top = lat == n_lat - 1
    up = (jnp.where(is_top, lat, lat + 1), jnp.where(is_top, n_lon - 1 - lon, lon))
    down = (jnp.where(lat == 0, lat, lat - 1), lon)
    barrier = pltpu.get_barrier_semaphore()
    for other in (right, left, up):
        pl.semaphore_signal(barrier, inc=1, device_id=other, device_id_type=MESH)

    @pl.when(lat > 0)
    def _():
        pl.semaphore_signal(barrier, inc=1, device_id=down, device_id_type=MESH)

    pl.semaphore_wait(barrier, jnp.where(lat > 0, 4, 3))

    def copy(src, dst, slot, to):
        return pltpu.make_async_remote_copy(
            src_ref=src,
            dst_ref=dst,
            send_sem=send.at[slot],
            recv_sem=recv.at[slot],
            device_id=to,
            device_id_type=MESH,
        )

    to_right = copy(vt.at[last], west, 0, right)
    to_left = copy(vt.at[0], east, 1, left)
    to_up = copy(north_edge, south, 2, up)
    to_fold = copy(north_edge, north, 3, up)

    @pl.when(is_top)
    def _():
        to_fold.start()

    @pl.when(jnp.logical_not(is_top))
    def _():
        to_up.start()

    @pl.when(lat > 0)
    def _():
        to_down_other = pltpu.make_async_remote_copy(
            src_ref=south_edge,
            dst_ref=north,
            send_sem=send.at[4],
            recv_sem=recv.at[3],
            device_id=down,
            device_id_type=MESH,
        )
        to_down_other.start()

    to_right.start()
    to_left.start()

    @pl.when(lat == 0)
    def _():
        south[...] = jnp.zeros_like(south)

    @pl.when(lat > 0)
    def _():
        to_up.wait_recv()

    to_fold.wait_recv()
    to_right.wait_recv()
    to_left.wait_recv()
    to_right.wait_send()
    to_left.wait_send()

    @pl.when(is_top)
    def _():
        to_fold.wait_send()

    @pl.when(jnp.logical_not(is_top))
    def _():
        to_up.wait_send()

    @pl.when(lat > 0)
    def _():
        pltpu.make_async_remote_copy(
            src_ref=south_edge,
            dst_ref=north,
            send_sem=send.at[4],
            recv_sem=recv.at[3],
            device_id=down,
            device_id_type=MESH,
        ).wait_send()


def field_kernel(
    top_ref, vt, before, after, west, east, south, north, lon_m, lat_m, f_ref, gram_ref, scr
):
    step = pl.program_id(0)
    steps = pl.num_programs(0)
    width, ny, columns = vt.shape
    half = columns // 2
    is_top = top_ref[0] == 1
    lon_t = lon_m[...].T
    lat_t = lat_m[...].T
    row = lax.broadcasted_iota(jnp.int32, (ny, 1), 0)
    iy = lax.broadcasted_iota(jnp.int32, (ny, ny), 0)
    ix = lax.broadcasted_iota(jnp.int32, (ny, ny), 1)
    band = (ix == iy + 1).astype(jnp.float32) - (ix == iy - 1).astype(jnp.float32)
    band = band.astype(jnp.bfloat16)
    nx = width * 3
    for at in range(width):
        x = step * width + at
        if at == 0:
            lower = jnp.where(step == 0, west[...], before[0])
        else:
            lower = vt[at - 1]
        if at == width - 1:
            upper = jnp.where(step == steps - 1, east[...], after[0])
        else:
            upper = vt[at + 1]
        over_x = upper.astype(jnp.float32) - lower.astype(jnp.float32)
        x_top = jnp.where(is_top, nx - 1 - x, x)
        above = north[pl.ds(x_top, 1), :]
        above = jnp.where(is_top, -above, above)
        below = south[pl.ds(x, 1), :]
        over_y = lax.dot_general(band, vt[at], NN, preferred_element_type=jnp.float32)
        over_y = over_y + jnp.where(row == ny - 1, above, 0.0) - jnp.where(row == 0, below, 0.0)
        m_lon = lon_t[:, at : at + 1]
        m_lat = lat_t[:, at : at + 1]
        zeta = m_lon * over_x[:, half:] - m_lat * over_y[:, :half]
        divergence = m_lon * over_x[:, :half] + m_lat * over_y[:, half:]
        f_ref[at * ny : (at + 1) * ny, :half] = zeta.astype(jnp.bfloat16)
        f_ref[at * ny : (at + 1) * ny, half:] = divergence.astype(jnp.bfloat16)
    part = lax.dot_general(f_ref[...], f_ref[...], TN, preferred_element_type=jnp.float32)

    @pl.when(step == 0)
    def _():
        scr[...] = part

    @pl.when(step > 0)
    def _():
        scr[...] += part

    @pl.when(step == steps - 1)
    def _():
        at = 0
        for i in range(4):
            for j in range(i, 4):
                gram_ref[at] = scr[i * 128 : (i + 1) * 128, j * 128 : (j + 1) * 128]
                at += 1


def sum_kernel(g, out, r0, s0, r1, r2, s1, r3, send0, recv0, send1, recv1, send2, recv2, send3, recv3, send4, recv4):
    lat, lon = lax.axis_index("lat"), lax.axis_index("lon")
    core, cx = lax.rem(lat, 2), lat // 2
    cy, cz = lon // 8, lax.rem(lon, 8)
    mine = cx * 4 + cy
    mate = (lat + 1 - 2 * core, lon)

    def plane(off):
        spot = lax.rem(mine + off, 16)
        return spot, (2 * (spot // 4) + core, 8 * lax.rem(spot, 4) + cz)

    def column(off):
        return (lat, 8 * cy + lax.rem(cz + off, 8))

    barrier = pltpu.get_barrier_semaphore()
    pl.semaphore_signal(barrier, inc=1, device_id=mate, device_id_type=MESH)
    for off in range(1, 16):
        pl.semaphore_signal(barrier, inc=1, device_id=plane(off)[1], device_id_type=MESH)
    for off in range(1, 8):
        pl.semaphore_signal(barrier, inc=1, device_id=column(off), device_id_type=MESH)
    pl.semaphore_wait(barrier, 23)

    def copy(src, dst, send, recv, to):
        return pltpu.make_async_remote_copy(
            src_ref=src, dst_ref=dst, send_sem=send, recv_sem=recv, device_id=to, device_id_type=MESH
        )

    first = copy(g.at[1 - core], r0, send0.at[0], recv0.at[0], mate)
    first.start()
    first.wait_recv()
    s0[...] = g[core] + r0[...]
    second = []
    for off in range(1, 16):
        spot, to = plane(off)
        second.append(copy(s0.at[spot], r1.at[mine], send1.at[off - 1], recv1.at[off - 1], to))
        second[-1].start()
    r1[mine] = s0[mine]
    for item in second:
        item.wait_recv()
    total = r1[0]
    for at in range(1, 16):
        total = total + r1[at]
    s1[0] = total
    r2[cz] = total
    third = []
    for off in range(1, 8):
        third.append(copy(s1.at[0], r2.at[cz], send2.at[off - 1], recv2.at[off - 1], column(off)))
        third[-1].start()
    for item in third:
        item.wait_recv()
    total = r2[0]
    for at in range(1, 8):
        total = total + r2[at]
    s1[1] = total
    r3[mine] = total
    fourth = []
    for off in range(1, 16):
        fourth.append(
            copy(s1.at[1], r3.at[mine], send3.at[off - 1], recv3.at[off - 1], plane(off)[1])
        )
        fourth[-1].start()
    for item in fourth:
        item.wait_recv()
    last = copy(r3, out.at[core], send4.at[0], recv4.at[0], mate)
    last.start()
    out[core] = r3[...]
    last.wait_recv()
    for item in [first, *second, *third, *fourth, last]:
        item.wait_send()


def pick_kernel(idx_ref, f_ref, o_ref, spread, picked):
    rows = f_ref.shape[0]
    lanes = f_ref.shape[1] // 4

    def widen(at, _):
        base = pl.multiple_of(at * 128, 128)
        for k in range(4):
            spread[pl.ds(base, 128), k, :] = f_ref[
                pl.ds(base, 128), k * lanes : (k + 1) * lanes
            ].astype(jnp.float32)
        return 0

    lax.fori_loop(0, rows // 128, widen, 0)

    def pick(at, _):
        base = at * 32
        for u in range(32):
            picked[base + u] = spread[idx_ref[base + u]]
        return 0

    lax.fori_loop(0, rows // 32, pick, 0)

    def narrow(at, _):
        base = pl.multiple_of(at * 128, 128)
        for k in range(4):
            o_ref[pl.ds(base, 128), k * lanes : (k + 1) * lanes] = picked[
                pl.ds(base, 128), k, :
            ].astype(jnp.bfloat16)
        return 0

    lax.fori_loop(0, rows // 128, narrow, 0)


def exact(a, b, dims):
    return lax.dot_general(
        a, b, dims, precision=lax.Precision.HIGHEST, preferred_element_type=jnp.float32
    )


def eliminate(a):
    n = a.shape[0]
    ri = lax.broadcasted_iota(jnp.int32, (n, n), 0)
    ci = lax.broadcasted_iota(jnp.int32, (n, n), 1)
    for k in range(n):
        row = a[k : k + 1, :]
        m = jnp.where(ri[:, :1] > k, a[:, k : k + 1] * (1.0 / a[k : k + 1, k : k + 1]), 0.0)
        rowz = jnp.where(ci[:1] == k, 1.0, row)
        a = jnp.where((ci == k) & (ri > k), 0.0, a) - m * rowz
    diagonal = jnp.sum(jnp.where(ri == ci, a, 0.0), axis=1, keepdims=True)
    root = lax.rsqrt(diagonal)
    upper = jnp.where(ri <= ci, a, 0.0) * root
    inverse = (jnp.where(ri > ci, a, 0.0) + jnp.where(ri == ci, 1.0, 0.0)) * root
    return upper, inverse


def factor_kernel(scale, g_ref, t_hbm, o_hbm, r_ref, rows, w_ref, stage, in_sem, out_sem):
    load = pltpu.make_async_copy(t_hbm, rows, in_sem)
    load.start()
    b = 128
    n = 4
    g = {}
    at = 0
    for i in range(n):
        for j in range(i, n):
            g[i, j] = g_ref[at]
            at += 1
    r, w = {}, {}
    for p in range(n):
        r[p, p], w[p, p] = eliminate(g[p, p])
        for j in range(p + 1, n):
            r[p, j] = exact(w[p, p], g[p, j], NN)
        for i in range(p + 1, n):
            for j in range(i, n):
                g[i, j] = g[i, j] - exact(r[p, i], r[p, j], TN)
    for i in range(n):
        for j in range(i):
            total = exact(r[j, i], w[j, j], TN)
            for k in range(j + 1, i):
                total = total + exact(r[k, i], w[k, j], TN)
            w[i, j] = -exact(w[i, i], total, NN)
    for i in range(n):
        for j in range(n):
            spot = (slice(i * b, (i + 1) * b), slice(j * b, (j + 1) * b))
            r_ref[spot] = r[i, j] * (1.0 / scale) if i <= j else jnp.zeros((b, b), jnp.float32)
            value = w[i, j] * scale if i >= j else jnp.zeros((b, b), jnp.float32)
            high = value.astype(jnp.bfloat16)
            w_ref[(0, *spot)] = high
            w_ref[(1, *spot)] = (value - high.astype(jnp.float32)).astype(jnp.bfloat16)
    load.wait()
    chunk = stage.shape[2]
    pieces = rows.shape[0] // chunk
    outs = []
    for at in range(pieces):
        slot = at % 2
        if at >= 2:
            outs[at - 2].wait()
        part = rows[at * chunk : (at + 1) * chunk, :]
        value = lax.dot_general(w_ref[0], part, NT, preferred_element_type=jnp.float32)
        value += lax.dot_general(w_ref[1], part, NT, preferred_element_type=jnp.float32)
        stage[slot] = value.astype(jnp.bfloat16)
        outs.append(
            pltpu.make_async_copy(
                stage.at[slot], o_hbm.at[:, pl.ds(at * chunk, chunk)], out_sem.at[slot]
            )
        )
        outs[-1].start()
    for item in outs[-2:]:
        item.wait()


def shards(n_lat, n_lon, velocity, lon_metric, lat_metric, wet_index, wet_count):
    days, nx, ny = velocity.shape[1:]
    cols = 2 * days
    cells = nx * ny
    f32, bf16 = jnp.float32, jnp.bfloat16
    shape = jax.ShapeDtypeStruct
    params = pltpu.CompilerParams(vmem_limit_bytes=BIG)

    lon_m, lat_m = pl.pallas_call(
        metric_kernel,
        in_specs=[VMEM, SMEM, VMEM, VMEM],
        out_specs=[VMEM, VMEM],
        out_shape=[shape((nx, ny), f32)] * 2,
        compiler_params=params,
    )(wet_index.reshape(6, -1), wet_count, lon_metric, lat_metric)

    lane = 128
    vt, north_edge, south_edge = pl.pallas_call(
        turn_kernel,
        grid=(cols // lane,),
        in_specs=[pl.BlockSpec((lane, nx, ny), lambda i: (i, 0, 0))],
        out_specs=[
            pl.BlockSpec((nx, ny, lane), lambda i: (0, 0, i)),
            pl.BlockSpec((nx, lane), lambda i: (0, i)),
            pl.BlockSpec((nx, lane), lambda i: (0, i)),
        ],
        out_shape=[shape((nx, ny, cols), bf16), shape((nx, cols), f32), shape((nx, cols), f32)],
        scratch_shapes=[pltpu.VMEM((lane, nx, ny), f32)],
        compiler_params=params,
    )(velocity.reshape(cols, nx, ny))

    west, east, south, north = pl.pallas_call(
        functools.partial(halo_kernel, n_lat, n_lon),
        in_specs=[ANY, ANY, ANY],
        out_specs=[VMEM] * 4,
        out_shape=[shape((ny, cols), bf16)] * 2 + [shape((nx, cols), f32)] * 2,
        scratch_shapes=[pltpu.SemaphoreType.DMA((5,)), pltpu.SemaphoreType.DMA((4,))],
        compiler_params=pltpu.CompilerParams(collective_id=0, has_side_effects=True),
    )(vt, north_edge, south_edge)

    is_top = (lax.axis_index("lat") == n_lat - 1).astype(jnp.int32).reshape(1)
    width = 16
    last = nx - 1
    whole = lambda a: pl.BlockSpec(a.shape, lambda i: (0,) * a.ndim)
    f, gram = pl.pallas_call(
        field_kernel,
        grid=(nx // width,),
        in_specs=[
            SMEM,
            pl.BlockSpec((width, ny, cols), lambda i: (i, 0, 0)),
            pl.BlockSpec((1, ny, cols), lambda i: (jnp.maximum(width * i - 1, 0), 0, 0)),
            pl.BlockSpec((1, ny, cols), lambda i: (jnp.minimum(width * i + width, last), 0, 0)),
            whole(west),
            whole(east),
            whole(south),
            whole(north),
            pl.BlockSpec((width, ny), lambda i: (i, 0)),
            pl.BlockSpec((width, ny), lambda i: (i, 0)),
        ],
        out_specs=[
            pl.BlockSpec((width * ny, cols), lambda i: (i, 0)),
            pl.BlockSpec((10, 128, 128), lambda i: (0, 0, 0)),
        ],
        out_shape=[shape((cells, cols), bf16), shape((10, 128, 128), f32)],
        scratch_shapes=[pltpu.VMEM((cols, cols), f32)],
        compiler_params=params,
    )(is_top, vt, vt, vt, west, east, south, north, lon_m, lat_m)

    dma = pltpu.SemaphoreType.DMA
    total = pl.pallas_call(
        sum_kernel,
        in_specs=[VMEM],
        out_specs=VMEM,
        out_shape=shape((2, 16, 40, 128), f32),
        scratch_shapes=[
            pltpu.VMEM((16, 40, 128), f32),
            pltpu.VMEM((16, 40, 128), f32),
            pltpu.VMEM((16, 40, 128), f32),
            pltpu.VMEM((8, 40, 128), f32),
            pltpu.VMEM((2, 40, 128), f32),
            pltpu.VMEM((16, 40, 128), f32),
            dma((1,)),
            dma((1,)),
            dma((15,)),
            dma((15,)),
            dma((7,)),
            dma((7,)),
            dma((15,)),
            dma((15,)),
            dma((1,)),
            dma((1,)),
        ],
        compiler_params=pltpu.CompilerParams(collective_id=1, has_side_effects=True),
    )(gram.reshape(2, 16, 40, 128))

    picked = pl.pallas_call(
        pick_kernel,
        in_specs=[SMEM, VMEM],
        out_specs=VMEM,
        out_shape=shape((cells, cols), bf16),
        scratch_shapes=[pltpu.VMEM((cells, 4, 128), f32), pltpu.VMEM((cells, 4, 128), f32)],
        compiler_params=params,
    )(wet_index, f)

    scale = math.sqrt(cells * n_lat * n_lon)
    basis, r_factor = pl.pallas_call(
        functools.partial(factor_kernel, scale),
        in_specs=[VMEM, ANY],
        out_specs=[ANY, VMEM],
        out_shape=[shape((cols, cells), bf16), shape((cols, cols), f32)],
        scratch_shapes=[
            pltpu.VMEM((cells, cols), bf16),
            pltpu.VMEM((2, cols, cols), bf16),
            pltpu.VMEM((2, cols, 768), bf16),
            dma(()),
            dma((2,)),
        ],
        compiler_params=params,
    )(total.reshape(10, 128, 128), picked)
    return basis, r_factor


def solution(mesh):
    n_lat, n_lon = mesh.shape["lat"], mesh.shape["lon"]
    placed = (
        P(None, None, "lon", "lat"),
        P("lon", "lat"),
        P("lon", "lat"),
        P(("lat", "lon")),
        P(("lat", "lon")),
    )
    return jax.shard_map(
        functools.partial(shards, n_lat, n_lon),
        mesh=mesh,
        in_specs=placed,
        out_specs=(P(None, ("lat", "lon")), P()),
        check_vma=False,
    )
```

```python
import functools
import math

import jax
import jax.numpy as jnp
from jax import lax
from jax.experimental import pallas as pl
from jax.experimental.pallas import tpu as pltpu
from jax.sharding import PartitionSpec as P

MESH = pl.DeviceIdType.MESH
VMEM = pl.BlockSpec(memory_space=pltpu.VMEM)
SMEM = pl.BlockSpec(memory_space=pltpu.SMEM)
ANY = pl.BlockSpec(memory_space=pl.ANY)
BIG = 60 << 20
NT = (((1,), (1,)), ((), ()))
TN = (((0,), (0,)), ((), ()))
NN = (((1,), (0,)), ((), ()))


def metric_kernel(idx_ref, count_ref, lon_ref, lat_ref, lon_out, lat_out):
    count = count_ref[0]
    pieces, width = idx_ref.shape
    nx, ny = lon_ref.shape
    total = jnp.zeros((nx, ny), jnp.float32)
    for at in range(pieces):
        cell = idx_ref[at : at + 1, :]
        place = lax.broadcasted_iota(jnp.int32, (1, width), 1) + at * width
        column = jnp.where(place < count, cell // ny, -1)
        row = cell % ny
        hot_x = (lax.broadcasted_iota(jnp.int32, (nx, width), 0) == column).astype(jnp.float32)
        hot_y = (lax.broadcasted_iota(jnp.int32, (ny, width), 0) == row).astype(jnp.float32)
        total += lax.dot_general(
            hot_x.astype(jnp.bfloat16),
            hot_y.astype(jnp.bfloat16),
            NT,
            preferred_element_type=jnp.float32,
        )
    lon_out[...] = 0.5 * lon_ref[...] * total
    lat_out[...] = 0.5 * lat_ref[...] * total


def turn_kernel(v_ref, o_ref, north_ref, south_ref, scr):
    scr[...] = v_ref[...].astype(jnp.float32)
    for x in range(v_ref.shape[1]):
        turned = scr[:, x, :].T
        o_ref[x] = turned.astype(jnp.bfloat16)
        north_ref[x : x + 1, :] = turned[-1:, :]
        south_ref[x : x + 1, :] = turned[:1, :]


def halo_kernel(n_lat, n_lon, vt, north_edge, south_edge, west, east, south, north, send, recv):
    lat, lon = lax.axis_index("lat"), lax.axis_index("lon")
    last = vt.shape[0] - 1
    right = (lat, lax.rem(lon + 1, n_lon))
    left = (lat, lax.rem(lon + n_lon - 1, n_lon))
    is_top = lat == n_lat - 1
    up = (jnp.where(is_top, lat, lat + 1), jnp.where(is_top, n_lon - 1 - lon, lon))
    down = (jnp.where(lat == 0, lat, lat - 1), lon)
    barrier = pltpu.get_barrier_semaphore()
    for other in (right, left, up):
        pl.semaphore_signal(barrier, inc=1, device_id=other, device_id_type=MESH)

    @pl.when(lat > 0)
    def _():
        pl.semaphore_signal(barrier, inc=1, device_id=down, device_id_type=MESH)

    pl.semaphore_wait(barrier, jnp.where(lat > 0, 4, 3))

    def copy(src, dst, slot, to):
        return pltpu.make_async_remote_copy(
            src_ref=src,
            dst_ref=dst,
            send_sem=send.at[slot],
            recv_sem=recv.at[slot],
            device_id=to,
            device_id_type=MESH,
        )

    to_right = copy(vt.at[last], west, 0, right)
    to_left = copy(vt.at[0], east, 1, left)
    to_up = copy(north_edge, south, 2, up)
    to_fold = copy(north_edge, north, 3, up)

    @pl.when(is_top)
    def _():
        to_fold.start()

    @pl.when(jnp.logical_not(is_top))
    def _():
        to_up.start()

    @pl.when(lat > 0)
    def _():
        to_down_other = pltpu.make_async_remote_copy(
            src_ref=south_edge,
            dst_ref=north,
            send_sem=send.at[4],
            recv_sem=recv.at[3],
            device_id=down,
            device_id_type=MESH,
        )
        to_down_other.start()

    to_right.start()
    to_left.start()

    @pl.when(lat == 0)
    def _():
        south[...] = jnp.zeros_like(south)

    @pl.when(lat > 0)
    def _():
        to_up.wait_recv()

    to_fold.wait_recv()
    to_right.wait_recv()
    to_left.wait_recv()
    to_right.wait_send()
    to_left.wait_send()

    @pl.when(is_top)
    def _():
        to_fold.wait_send()

    @pl.when(jnp.logical_not(is_top))
    def _():
        to_up.wait_send()

    @pl.when(lat > 0)
    def _():
        pltpu.make_async_remote_copy(
            src_ref=south_edge,
            dst_ref=north,
            send_sem=send.at[4],
            recv_sem=recv.at[3],
            device_id=down,
            device_id_type=MESH,
        ).wait_send()


def field_kernel(
    top_ref, vt, before, after, west, east, south, north, lon_m, lat_m, f_ref, gram_ref, scr
):
    step = pl.program_id(0)
    steps = pl.num_programs(0)
    width, ny, columns = vt.shape
    half = columns // 2
    is_top = top_ref[0] == 1
    lon_t = lon_m[...].T
    lat_t = lat_m[...].T
    row = lax.broadcasted_iota(jnp.int32, (ny, 1), 0)
    iy = lax.broadcasted_iota(jnp.int32, (ny, ny), 0)
    ix = lax.broadcasted_iota(jnp.int32, (ny, ny), 1)
    band = (ix == iy + 1).astype(jnp.float32) - (ix == iy - 1).astype(jnp.float32)
    band = band.astype(jnp.bfloat16)
    nx = width * 3
    for at in range(width):
        x = step * width + at
        if at == 0:
            lower = jnp.where(step == 0, west[...], before[0])
        else:
            lower = vt[at - 1]
        if at == width - 1:
            upper = jnp.where(step == steps - 1, east[...], after[0])
        else:
            upper = vt[at + 1]
        over_x = upper.astype(jnp.float32) - lower.astype(jnp.float32)
        x_top = jnp.where(is_top, nx - 1 - x, x)
        above = north[pl.ds(x_top, 1), :]
        above = jnp.where(is_top, -above, above)
        below = south[pl.ds(x, 1), :]
        over_y = lax.dot_general(band, vt[at], NN, preferred_element_type=jnp.float32)
        over_y = over_y + jnp.where(row == ny - 1, above, 0.0) - jnp.where(row == 0, below, 0.0)
        m_lon = lon_t[:, at : at + 1]
        m_lat = lat_t[:, at : at + 1]
        zeta = m_lon * over_x[:, half:] - m_lat * over_y[:, :half]
        divergence = m_lon * over_x[:, :half] + m_lat * over_y[:, half:]
        f_ref[at * ny : (at + 1) * ny, :half] = zeta.astype(jnp.bfloat16)
        f_ref[at * ny : (at + 1) * ny, half:] = divergence.astype(jnp.bfloat16)
    part = lax.dot_general(f_ref[...], f_ref[...], TN, preferred_element_type=jnp.float32)

    @pl.when(step == 0)
    def _():
        scr[...] = part

    @pl.when(step > 0)
    def _():
        scr[...] += part

    @pl.when(step == steps - 1)
    def _():
        at = 0
        for i in range(4):
            for j in range(i, 4):
                gram_ref[at] = scr[i * 128 : (i + 1) * 128, j * 128 : (j + 1) * 128]
                at += 1


def sum_kernel(
    idx, g, f_hbm, out, t_hbm, rows, spread, picked, r0, s0, r1, r2, s1, r3,
    send0, recv0, send1, recv1, send2, recv2, send3, recv3, send4, recv4, load_sem, store_sem,
):
    lat, lon = lax.axis_index("lat"), lax.axis_index("lon")
    core, cx = lax.rem(lat, 2), lat // 2
    cy, cz = lon // 8, lax.rem(lon, 8)
    mine = cx * 4 + cy
    mate = (lat + 1 - 2 * core, lon)
    cells, cols = rows.shape
    piece = cells // 4

    def plane(off):
        spot = lax.rem(mine + off, 16)
        return spot, (2 * (spot // 4) + core, 8 * lax.rem(spot, 4) + cz)

    def column(off):
        return (lat, 8 * cy + lax.rem(cz + off, 8))

    def widen(at, _):
        here = pl.ds(pl.multiple_of(at * 128, 128), 128)
        spread[here] = rows[here, :].astype(jnp.float32).reshape(128, 4, cols // 4)
        return 0

    def pick(at, _):
        base = at * 64
        taken = [spread[idx[base + u]] for u in range(64)]
        for u in range(64):
            picked[base + u] = taken[u]
        return 0

    def narrow(at, _):
        here = pl.ds(pl.multiple_of(at * 128, 128), 128)
        rows[here, :] = picked[here].reshape(128, cols).astype(jnp.bfloat16)
        return 0

    def pick_piece(at):
        lax.fori_loop(at * piece // 64, (at + 1) * piece // 64, pick, 0)

    def store_piece(at):
        lax.fori_loop(at * piece // 128, (at + 1) * piece // 128, narrow, 0)
        here = pl.ds(at * piece, piece)
        item = pltpu.make_async_copy(rows.at[here], t_hbm.at[here], store_sem.at[at])
        item.start()
        return item

    load = pltpu.make_async_copy(f_hbm, rows, load_sem)
    load.start()
    barrier = pltpu.get_barrier_semaphore()
    pl.semaphore_signal(barrier, inc=1, device_id=mate, device_id_type=MESH)
    for off in range(1, 16):
        pl.semaphore_signal(barrier, inc=1, device_id=plane(off)[1], device_id_type=MESH)
    for off in range(1, 8):
        pl.semaphore_signal(barrier, inc=1, device_id=column(off), device_id_type=MESH)
    pl.semaphore_wait(barrier, 23)

    def copy(src, dst, send, recv, to):
        return pltpu.make_async_remote_copy(
            src_ref=src, dst_ref=dst, send_sem=send, recv_sem=recv, device_id=to, device_id_type=MESH
        )

    first = copy(g.at[1 - core], r0, send0.at[0], recv0.at[0], mate)
    first.start()
    first.wait_recv()
    s0[...] = g[core] + r0[...]
    second = []
    for off in range(1, 16):
        spot, to = plane(off)
        second.append(copy(s0.at[spot], r1.at[mine], send1.at[off - 1], recv1.at[off - 1], to))
        second[-1].start()
    r1[mine] = s0[mine]
    load.wait()
    lax.fori_loop(0, cells // 128, widen, 0)
    pick_piece(0)
    for item in second:
        item.wait_recv()
    total = r1[0]
    for at in range(1, 16):
        total = total + r1[at]
    s1[0] = total
    r2[cz] = total
    third = []
    for off in range(1, 8):
        third.append(copy(s1.at[0], r2.at[cz], send2.at[off - 1], recv2.at[off - 1], column(off)))
        third[-1].start()
    pick_piece(1)
    pick_piece(2)
    for item in third:
        item.wait_recv()
    total = r2[0]
    for at in range(1, 8):
        total = total + r2[at]
    s1[1] = total
    r3[mine] = total
    fourth = []
    for off in range(1, 16):
        fourth.append(
            copy(s1.at[1], r3.at[mine], send3.at[off - 1], recv3.at[off - 1], plane(off)[1])
        )
        fourth[-1].start()
    pick_piece(3)
    stores = [store_piece(at) for at in range(4)]
    for item in fourth:
        item.wait_recv()
    last = copy(r3, out.at[core], send4.at[0], recv4.at[0], mate)
    last.start()
    out[core] = r3[...]
    last.wait_recv()
    for item in stores:
        item.wait()
    for item in [first, *second, *third, *fourth, last]:
        item.wait_send()


def exact(a, b, dims):
    return lax.dot_general(
        a, b, dims, precision=lax.Precision.HIGHEST, preferred_element_type=jnp.float32
    )


def tree(terms):
    while len(terms) > 1:
        odd = terms[-1:] if len(terms) % 2 else []
        terms = [p + q for p, q in zip(terms[0::2], terms[1::2])] + odd
    return terms[0]


def eliminate(a):
    n = a.shape[0]
    b = 8
    rows = [a[b * i : b * i + b, :] for i in range(n // b)]
    ci = lax.broadcasted_iota(jnp.int32, (b, n), 1)
    ri = lax.broadcasted_iota(jnp.int32, (b, n), 0)
    unit = [jnp.where(ri == j, 1.0, 0.0) for j in range(b)]

    def lane(v, c):
        return jnp.broadcast_to(v[:, c : c + 1], (b, n))

    pivot = [lane(rows[0], j) for j in range(b)]
    uppers, inverses = [], []
    for p in range(n // b):
        q = rows[p]
        x = list(unit)
        inside = (ci >= b * p) & (ci < b * p + b)
        q1 = jnp.where(inside, jnp.where(ci - b * p == ri, 1.0, 0.0), q)
        more = p + 1 < n // b
        if more:
            below = rows[p + 1]
            below_old = [lane(below, b * p + j) for j in range(b)]
            below_new = [lane(below, b * p + b + j) for j in range(b)]
            ahead = [lane(q, b * p + b + j) for j in range(b)]
        for k in range(b):
            value = jnp.broadcast_to(pivot[k][k : k + 1, :], (b, n))
            inv = 1.0 / value
            root = lax.rsqrt(value)
            col = jnp.where(ri == k, 0.0, pivot[k])
            fac = jnp.where(ri == k, -1.0, pivot[k])
            col_inv = col * inv
            under = jnp.where(ri > k, col_inv, 0.0)
            fresh = []
            for j in range(b):
                if j == k:
                    fresh.append(jnp.where(ri == k, inv, -col_inv))
                else:
                    fresh.append(
                        jnp.where(ri == k, 0.0, pivot[j]) - (fac * pivot[j][k : k + 1, :]) * inv
                    )
            pivot = fresh
            gain = jnp.where(ri == k, root, 1.0)
            for j in range(k + 1):
                x[j] = (x[j] - under * x[j][k : k + 1, :]) * gain
        z = tree([pivot[j] * q1[j : j + 1, :] for j in range(b)])
        if more:
            pivot_next = []
            for c in range(b):
                part = tree([pivot[j] * ahead[c][j : j + 1, :] for j in range(b)])
                pivot_next.append(
                    below_new[c] - tree([below_old[k] * part[k : k + 1, :] for k in range(b)])
                )
        z_rows = [jnp.broadcast_to(z[j : j + 1, :], (b, n)) for j in range(b)]
        for i in range(p + 1, n // b):
            src = rows[i]
            rows[i] = jnp.where(inside, 0.0, src) - tree(
                [lane(src, b * p + j) * z_rows[j] for j in range(b)]
            )
        upper = tree([x[j] * q[j : j + 1, :] for j in range(b)])
        inverse = tree([x[j] * q1[j : j + 1, :] for j in range(b)])
        diag = ci - b * p >= ri
        uppers.append(jnp.where(diag, upper, 0.0))
        inverses.append(jnp.where(ci - b * p <= ri, inverse, 0.0))
        if more:
            pivot = pivot_next
    return jnp.concatenate(uppers, axis=0), jnp.concatenate(inverses, axis=0)


def factor_kernel(scale, g_ref, t_hbm, o_hbm, r_ref, rows, w_ref, stage, in_sem, out_sem):
    load = pltpu.make_async_copy(t_hbm, rows, in_sem)
    load.start()
    b = 128
    n = 4
    g = {}
    at = 0
    for i in range(n):
        for j in range(i, n):
            g[i, j] = g_ref[at]
            at += 1
    r, w = {}, {}
    for p in range(n):
        held = {}
        for j in range(p):
            held[j] = tree([exact(r[k, p], w[k, j], TN) for k in range(j, p)])
        r[p, p], w[p, p] = eliminate(g[p, p])
        if p + 1 < n:
            ahead = exact(w[p, p], jnp.concatenate([g[p, j] for j in range(p + 1, n)], axis=1), NN)
            for j in range(p + 1, n):
                r[p, j] = ahead[:, (j - p - 1) * b : (j - p) * b]
        for i in range(p + 1, n):
            for j in range(i, n):
                g[i, j] = g[i, j] - exact(r[p, i], r[p, j], TN)
        if p:
            behind = exact(w[p, p], jnp.concatenate([held[j] for j in range(p)], axis=1), NN)
            for j in range(p):
                w[p, j] = -behind[:, j * b : (j + 1) * b]
    for i in range(n):
        for j in range(n):
            spot = (slice(i * b, (i + 1) * b), slice(j * b, (j + 1) * b))
            r_ref[spot] = r[i, j] * (1.0 / scale) if i <= j else jnp.zeros((b, b), jnp.float32)
            value = w[i, j] * scale if i >= j else jnp.zeros((b, b), jnp.float32)
            high = value.astype(jnp.bfloat16)
            w_ref[(0, *spot)] = high
            w_ref[(1, *spot)] = (value - high.astype(jnp.float32)).astype(jnp.bfloat16)
    load.wait()
    chunk = stage.shape[2]
    pieces = rows.shape[0] // chunk
    outs = []
    for at in range(pieces):
        slot = at % 2
        if at >= 2:
            outs[at - 2].wait()
        part = rows[at * chunk : (at + 1) * chunk, :]
        for top, end in ((0, 256), (256, 512)):
            value = tree(
                [
                    lax.dot_general(
                        w_ref[k, top:end, :end],
                        part[:, :end],
                        NT,
                        preferred_element_type=jnp.float32,
                    )
                    for k in range(2)
                ]
            )
            stage[slot, top:end] = value.astype(jnp.bfloat16)
        outs.append(
            pltpu.make_async_copy(
                stage.at[slot], o_hbm.at[:, pl.ds(at * chunk, chunk)], out_sem.at[slot]
            )
        )
        outs[-1].start()
    for item in outs[-2:]:
        item.wait()


def shards(n_lat, n_lon, velocity, lon_metric, lat_metric, wet_index, wet_count):
    days, nx, ny = velocity.shape[1:]
    cols = 2 * days
    cells = nx * ny
    f32, bf16 = jnp.float32, jnp.bfloat16
    shape = jax.ShapeDtypeStruct
    params = pltpu.CompilerParams(vmem_limit_bytes=BIG)

    lon_m, lat_m = pl.pallas_call(
        metric_kernel,
        in_specs=[VMEM, SMEM, VMEM, VMEM],
        out_specs=[VMEM, VMEM],
        out_shape=[shape((nx, ny), f32)] * 2,
        compiler_params=params,
    )(wet_index.reshape(6, -1), wet_count, lon_metric, lat_metric)

    lane = 128
    vt, north_edge, south_edge = pl.pallas_call(
        turn_kernel,
        grid=(cols // lane,),
        in_specs=[pl.BlockSpec((lane, nx, ny), lambda i: (i, 0, 0))],
        out_specs=[
            pl.BlockSpec((nx, ny, lane), lambda i: (0, 0, i)),
            pl.BlockSpec((nx, lane), lambda i: (0, i)),
            pl.BlockSpec((nx, lane), lambda i: (0, i)),
        ],
        out_shape=[shape((nx, ny, cols), bf16), shape((nx, cols), f32), shape((nx, cols), f32)],
        scratch_shapes=[pltpu.VMEM((lane, nx, ny), f32)],
        compiler_params=params,
    )(velocity.reshape(cols, nx, ny))

    west, east, south, north = pl.pallas_call(
        functools.partial(halo_kernel, n_lat, n_lon),
        in_specs=[ANY, ANY, ANY],
        out_specs=[VMEM] * 4,
        out_shape=[shape((ny, cols), bf16)] * 2 + [shape((nx, cols), f32)] * 2,
        scratch_shapes=[pltpu.SemaphoreType.DMA((5,)), pltpu.SemaphoreType.DMA((4,))],
        compiler_params=pltpu.CompilerParams(collective_id=0, has_side_effects=True),
    )(vt, north_edge, south_edge)

    is_top = (lax.axis_index("lat") == n_lat - 1).astype(jnp.int32).reshape(1)
    width = 16
    last = nx - 1
    whole = lambda a: pl.BlockSpec(a.shape, lambda i: (0,) * a.ndim)
    f, gram = pl.pallas_call(
        field_kernel,
        grid=(nx // width,),
        in_specs=[
            SMEM,
            pl.BlockSpec((width, ny, cols), lambda i: (i, 0, 0)),
            pl.BlockSpec((1, ny, cols), lambda i: (jnp.maximum(width * i - 1, 0), 0, 0)),
            pl.BlockSpec((1, ny, cols), lambda i: (jnp.minimum(width * i + width, last), 0, 0)),
            whole(west),
            whole(east),
            whole(south),
            whole(north),
            pl.BlockSpec((width, ny), lambda i: (i, 0)),
            pl.BlockSpec((width, ny), lambda i: (i, 0)),
        ],
        out_specs=[
            pl.BlockSpec((width * ny, cols), lambda i: (i, 0)),
            pl.BlockSpec((10, 128, 128), lambda i: (0, 0, 0)),
        ],
        out_shape=[shape((cells, cols), bf16), shape((10, 128, 128), f32)],
        scratch_shapes=[pltpu.VMEM((cols, cols), f32)],
        compiler_params=params,
    )(is_top, vt, vt, vt, west, east, south, north, lon_m, lat_m)

    dma = pltpu.SemaphoreType.DMA
    total, picked = pl.pallas_call(
        sum_kernel,
        in_specs=[SMEM, VMEM, ANY],
        out_specs=[VMEM, ANY],
        out_shape=[shape((2, 16, 40, 128), f32), shape((cells, cols), bf16)],
        scratch_shapes=[
            pltpu.VMEM((cells, cols), bf16),
            pltpu.VMEM((cells, 4, cols // 4), f32),
            pltpu.VMEM((cells, 4, cols // 4), f32),
            pltpu.VMEM((16, 40, 128), f32),
            pltpu.VMEM((16, 40, 128), f32),
            pltpu.VMEM((16, 40, 128), f32),
            pltpu.VMEM((8, 40, 128), f32),
            pltpu.VMEM((2, 40, 128), f32),
            pltpu.VMEM((16, 40, 128), f32),
            *[dma((n,)) for n in (1, 1, 15, 15, 7, 7, 15, 15, 1, 1)],
            dma(()),
            dma((4,)),
        ],
        compiler_params=pltpu.CompilerParams(
            collective_id=1, has_side_effects=True, vmem_limit_bytes=BIG
        ),
    )(wet_index, gram.reshape(2, 16, 40, 128), f)

    scale = math.sqrt(cells * n_lat * n_lon)
    basis, r_factor = pl.pallas_call(
        functools.partial(factor_kernel, scale),
        in_specs=[VMEM, ANY],
        out_specs=[ANY, VMEM],
        out_shape=[shape((cols, cells), bf16), shape((cols, cols), f32)],
        scratch_shapes=[
            pltpu.VMEM((cells, cols), bf16),
            pltpu.VMEM((2, cols, cols), bf16),
            pltpu.VMEM((2, cols, 1024), bf16),
            dma(()),
            dma((2,)),
        ],
        compiler_params=params,
    )(total.reshape(10, 128, 128), picked)
    return basis, r_factor


def solution(mesh):
    n_lat, n_lon = mesh.shape["lat"], mesh.shape["lon"]
    placed = (
        P(None, None, "lon", "lat"),
        P("lon", "lat"),
        P("lon", "lat"),
        P(("lat", "lon")),
        P(("lat", "lon")),
    )
    return jax.shard_map(
        functools.partial(shards, n_lat, n_lon),
        mesh=mesh,
        in_specs=placed,
        out_specs=(P(None, ("lat", "lon")), P()),
        check_vma=False,
    )
```

```python
import functools
import math

import jax
import jax.numpy as jnp
from jax import lax
from jax.experimental import pallas as pl
from jax.experimental.pallas import tpu as pltpu
from jax.sharding import PartitionSpec as P

MESH = pl.DeviceIdType.MESH
VMEM = pl.BlockSpec(memory_space=pltpu.VMEM)
SMEM = pl.BlockSpec(memory_space=pltpu.SMEM)
ANY = pl.BlockSpec(memory_space=pl.ANY)
BIG = 60 << 20
PIECE = 1536
NT = (((1,), (1,)), ((), ()))
TN = (((0,), (0,)), ((), ()))
NN = (((1,), (0,)), ((), ()))


def field_kernel(
    n_lat, n_lon, idx, count, lon_ref, lat_ref, v_hbm, f_hbm, gram_ref,
    vin, wide, vt, f, lon_t, lat_t, acc, edge, edge16, from16, south, north,
    load_sem, store_sem, send, recv,
):
    lat, lon = lax.axis_index("lat"), lax.axis_index("lon")
    nx, ny = lon_ref.shape
    lane = vin.shape[1]
    top = lat // (n_lat - 1)
    is_top = lat == n_lat - 1
    right = (lat, lax.rem(lon + 1, n_lon))
    left = (lat, lax.rem(lon + n_lon - 1, n_lon))
    up = (lat + 1 - top, lon + top * (n_lon - 1 - 2 * lon))
    down = (jnp.where(lat == 0, lat, lat - 1), lon)

    def load(step):
        c = lax.rem(step, 2) * 2 + step // 2
        return pltpu.make_async_copy(
            v_hbm.at[pl.ds(c * lane, lane)], vin.at[lax.rem(step, 2)], load_sem.at[lax.rem(step, 2)]
        )

    load(0).start()
    barrier = pltpu.get_barrier_semaphore()
    for other in (right, left, up):
        pl.semaphore_signal(barrier, inc=1, device_id=other, device_id_type=MESH)

    @pl.when(lat > 0)
    def _():
        pl.semaphore_signal(barrier, inc=1, device_id=down, device_id_type=MESH)

    live = count[0]
    total = jnp.zeros((nx, ny), jnp.float32)
    width = 8 * ny
    for at in range(nx // 8):
        cell = jnp.concatenate([idx[8 * at + i : 8 * at + i + 1, :] for i in range(8)], axis=1)
        place = lax.broadcasted_iota(jnp.int32, (1, width), 1) + at * width
        column = jnp.where(place < live, cell // ny, -1)
        hot_x = lax.broadcasted_iota(jnp.int32, (nx, width), 0) == column
        hot_y = lax.broadcasted_iota(jnp.int32, (ny, width), 0) == cell % ny
        total += lax.dot_general(
            hot_x.astype(jnp.float32).astype(jnp.bfloat16),
            hot_y.astype(jnp.float32).astype(jnp.bfloat16),
            NT,
            preferred_element_type=jnp.float32,
        )
    lon_m = 0.5 * lon_ref[...] * total
    lat_m = 0.5 * lat_ref[...] * total
    group = lon_t.shape[2]
    for at in range(nx // group):
        lon_t[at] = lon_m[at * group : (at + 1) * group].T
        lat_t[at] = lat_m[at * group : (at + 1) * group].T
    pl.semaphore_wait(barrier, jnp.where(lat > 0, 4, 3))

    def copy(src, dst, c, out, into, to):
        return pltpu.make_async_remote_copy(
            src_ref=src,
            dst_ref=dst,
            send_sem=send.at[c, out],
            recv_sem=recv.at[c, into],
            device_id=to,
            device_id_type=MESH,
        )

    def lanes(c):
        return pl.ds(pl.multiple_of(c * lane, lane), lane)

    def to_right(c):
        return copy(vt.at[nx, :, lanes(c)], vt.at[0, :, lanes(c)], c, 0, 0, right)

    def to_left(c):
        return copy(vt.at[1, :, lanes(c)], vt.at[nx + 1, :, lanes(c)], c, 1, 1, left)

    def to_up(c):
        return copy(edge16.at[1, c], from16.at[0, c], c, 2, 2, up)

    def to_fold(c):
        return copy(edge16.at[1, c], from16.at[1, c], c, 2, 3, up)

    def to_down(c):
        return copy(edge16.at[0, c], from16.at[1, c], c, 3, 3, down)

    def turn(step, _):
        c = lax.rem(step, 2) * 2 + step // 2
        load(step).wait()

        @pl.when(step < 3)
        def _():
            load(step + 1).start()

        wide[...] = vin[lax.rem(step, 2)].astype(jnp.float32)
        for x in range(nx):
            turned = wide[:, x, :].T
            vt[x + 1, :, lanes(c)] = turned.astype(jnp.bfloat16)
            edge[0, x : x + 1, :] = turned[:1, :]
            edge[1, x : x + 1, :] = turned[-1:, :]
        edge16[0, c] = edge[0].astype(jnp.bfloat16)
        edge16[1, c] = edge[1].astype(jnp.bfloat16)

        @pl.when(is_top)
        def _():
            to_fold(c).start()

        @pl.when(jnp.logical_not(is_top))
        def _():
            to_up(c).start()

        @pl.when(lat > 0)
        def _():
            to_down(c).start()

        to_right(c).start()
        to_left(c).start()
        return 0

    lax.fori_loop(0, 4, turn, 0)

    row = lax.broadcasted_iota(jnp.int32, (ny, 1), 0)
    iy = lax.broadcasted_iota(jnp.int32, (ny, ny), 0)
    ix = lax.broadcasted_iota(jnp.int32, (ny, ny), 1)
    band = (ix == iy + 1).astype(jnp.float32) - (ix == iy - 1).astype(jnp.float32)
    band = band.astype(jnp.bfloat16)
    acc[...] = jnp.zeros_like(acc)

    for h in range(2):
        for c in (h, 2 + h):
            to_right(c).wait_recv()
            to_left(c).wait_recv()
            to_fold(c).wait_recv()
            arrived = from16[1, c].astype(jnp.float32)
            north[c] = jnp.where(is_top, -arrived, arrived)

            @pl.when(lat == 0)
            def _():
                south[c] = jnp.zeros((nx, lane), jnp.float32)

            @pl.when(lat > 0)
            def _():
                to_up(c).wait_recv()
                south[c] = from16[0, c].astype(jnp.float32)

        cu, cv = h, 2 + h
        lu, lv = slice(cu * lane, cu * lane + lane), slice(cv * lane, cv * lane + lane)

        def fields(at_group, _):
            m_lon, m_lat = lon_t[at_group], lat_t[at_group]
            for at in range(group):
                x = at_group * group + at
                x_top = x + top * (nx - 1 - 2 * x)
                here = pl.ds(pl.multiple_of(x * ny, ny), ny)
                a, b = m_lon[:, at : at + 1], m_lat[:, at : at + 1]
                u_x = vt[x + 2, :, lu].astype(jnp.float32) - vt[x, :, lu].astype(jnp.float32)
                v_x = vt[x + 2, :, lv].astype(jnp.float32) - vt[x, :, lv].astype(jnp.float32)

                def over_y(c, where):
                    inner = lax.dot_general(
                        band, vt[x + 1, :, where], NN, preferred_element_type=jnp.float32
                    )
                    inner = inner + jnp.where(row == ny - 1, north[c, pl.ds(x_top, 1), :], 0.0)
                    return inner - jnp.where(row == 0, south[c, pl.ds(x, 1), :], 0.0)

                f[here, lu] = (a * v_x - b * over_y(cu, lu)).astype(jnp.bfloat16)
                f[here, lv] = (a * u_x + b * over_y(cv, lv)).astype(jnp.bfloat16)
            if h == 1:
                span = pl.ds(pl.multiple_of(at_group * (group * ny), group * ny), group * ny)
                pltpu.make_async_copy(f.at[span], f_hbm.at[span], store_sem.at[at_group]).start()
                acc[...] += lax.dot_general(
                    f[span, :], f[span, :], TN, preferred_element_type=jnp.float32
                )
            return 0

        lax.fori_loop(0, nx // group, fields, 0)
    at = 0
    for i in range(4):
        for j in range(i, 4):
            gram_ref[at] = acc[i * 128 : (i + 1) * 128, j * 128 : (j + 1) * 128]
            at += 1
    for at in range(nx // group):
        span = pl.ds(at * group * ny, group * ny)
        pltpu.make_async_copy(f.at[span], f_hbm.at[span], store_sem.at[at]).wait()
    for c in range(4):
        to_right(c).wait_send()
        to_left(c).wait_send()

        @pl.when(is_top)
        def _():
            to_fold(c).wait_send()

        @pl.when(jnp.logical_not(is_top))
        def _():
            to_up(c).wait_send()

        @pl.when(lat > 0)
        def _():
            to_down(c).wait_send()


def sum_kernel(
    idx, g, f_hbm, out, t_hbm, rows, spread, picked, r0, s0, r1, r2, s1, r3,
    send0, recv0, send1, recv1, send2, recv2, send3, recv3, send4, recv4, load_sem, store_sem,
):
    lat, lon = lax.axis_index("lat"), lax.axis_index("lon")
    core, cx = lax.rem(lat, 2), lat // 2
    cy, cz = lon // 8, lax.rem(lon, 8)
    mine = cx * 4 + cy
    mate = (lat + 1 - 2 * core, lon)
    cells, cols = rows.shape
    piece = cells // 4

    def plane(off):
        spot = lax.rem(mine + off, 16)
        return spot, (2 * (spot // 4) + core, 8 * lax.rem(spot, 4) + cz)

    def column(off):
        return (lat, 8 * cy + lax.rem(cz + off, 8))

    def widen(at, _):
        here = pl.ds(pl.multiple_of(at * 128, 128), 128)
        spread[here] = rows[here, :].astype(jnp.float32).reshape(128, 4, cols // 4)
        return 0

    def pick(at, _):
        base = at * 64
        taken = [spread[idx[base + u]] for u in range(64)]
        for u in range(64):
            picked[base + u] = taken[u]
        return 0

    def narrow(at, _):
        here = pl.ds(pl.multiple_of(at * 128, 128), 128)
        rows[here, :] = picked[here].reshape(128, cols).astype(jnp.bfloat16)
        return 0

    def pick_piece(at):
        lax.fori_loop(at * piece // 64, (at + 1) * piece // 64, pick, 0)

    def store_piece(at):
        lax.fori_loop(at * piece // 128, (at + 1) * piece // 128, narrow, 0)
        here = pl.ds(at * piece, piece)
        item = pltpu.make_async_copy(rows.at[here], t_hbm.at[here], store_sem.at[at])
        item.start()
        return item

    load = pltpu.make_async_copy(f_hbm, rows, load_sem)
    load.start()
    barrier = pltpu.get_barrier_semaphore()
    pl.semaphore_signal(barrier, inc=1, device_id=mate, device_id_type=MESH)
    for off in range(1, 16):
        pl.semaphore_signal(barrier, inc=1, device_id=plane(off)[1], device_id_type=MESH)
    for off in range(1, 8):
        pl.semaphore_signal(barrier, inc=1, device_id=column(off), device_id_type=MESH)
    pl.semaphore_wait(barrier, 23)

    def copy(src, dst, send, recv, to):
        return pltpu.make_async_remote_copy(
            src_ref=src, dst_ref=dst, send_sem=send, recv_sem=recv, device_id=to, device_id_type=MESH
        )

    first = copy(g.at[1 - core], r0, send0.at[0], recv0.at[0], mate)
    first.start()
    first.wait_recv()
    s0[...] = g[core] + r0[...]
    second = []
    for off in range(1, 16):
        spot, to = plane(off)
        second.append(copy(s0.at[spot], r1.at[mine], send1.at[off - 1], recv1.at[off - 1], to))
        second[-1].start()
    r1[mine] = s0[mine]
    load.wait()
    lax.fori_loop(0, cells // 128, widen, 0)
    pick_piece(0)
    for item in second:
        item.wait_recv()
    total = r1[0]
    for at in range(1, 16):
        total = total + r1[at]
    s1[0] = total
    r2[cz] = total
    third = []
    for off in range(1, 8):
        third.append(copy(s1.at[0], r2.at[cz], send2.at[off - 1], recv2.at[off - 1], column(off)))
        third[-1].start()
    pick_piece(1)
    pick_piece(2)
    for item in third:
        item.wait_recv()
    total = r2[0]
    for at in range(1, 8):
        total = total + r2[at]
    s1[1] = total
    r3[mine] = total
    fourth = []
    for off in range(1, 16):
        fourth.append(
            copy(s1.at[1], r3.at[mine], send3.at[off - 1], recv3.at[off - 1], plane(off)[1])
        )
        fourth[-1].start()
    pick_piece(3)
    stores = [store_piece(at) for at in range(4)]
    for item in fourth:
        item.wait_recv()
    last = copy(r3, out.at[core], send4.at[0], recv4.at[0], mate)
    last.start()
    out[core] = r3[...]
    last.wait_recv()
    for item in stores:
        item.wait()
    for item in [first, *second, *third, *fourth, last]:
        item.wait_send()


def exact(a, b, dims):
    return lax.dot_general(
        a, b, dims, precision=lax.Precision.HIGHEST, preferred_element_type=jnp.float32
    )


def tree(terms):
    while len(terms) > 1:
        odd = terms[-1:] if len(terms) % 2 else []
        terms = [p + q for p, q in zip(terms[0::2], terms[1::2])] + odd
    return terms[0]


def eliminate(a, beside):
    n = a.shape[0]
    b = 8
    rows = [a[b * i : b * i + b, :] for i in range(n // b)]
    ci = lax.broadcasted_iota(jnp.int32, (b, n), 1)
    ri = lax.broadcasted_iota(jnp.int32, (b, n), 0)
    unit = [jnp.where(ri == j, 1.0, 0.0) for j in range(b)]

    def lane(v, c):
        return jnp.broadcast_to(v[:, c : c + 1], (b, n))

    pivot = [lane(rows[0], j) for j in range(b)]
    uppers, inverses = [], []
    for p in range(n // b):
        q = rows[p]
        x = list(unit)
        inside = (ci >= b * p) & (ci < b * p + b)
        q1 = jnp.where(inside, jnp.where(ci - b * p == ri, 1.0, 0.0), q)
        more = p + 1 < n // b
        if more:
            below = rows[p + 1]
            below_old = [lane(below, b * p + j) for j in range(b)]
            below_new = [lane(below, b * p + b + j) for j in range(b)]
            ahead = [lane(q, b * p + b + j) for j in range(b)]
        for k in range(b):
            value = jnp.broadcast_to(pivot[k][k : k + 1, :], (b, n))
            inv = 1.0 / value
            root = lax.rsqrt(value)
            col = jnp.where(ri == k, 0.0, pivot[k])
            fac = jnp.where(ri == k, -1.0, pivot[k])
            col_inv = col * inv
            under = jnp.where(ri > k, col_inv, 0.0)
            fresh = []
            for j in range(b):
                if j == k:
                    fresh.append(jnp.where(ri == k, inv, -col_inv))
                else:
                    fresh.append(
                        jnp.where(ri == k, 0.0, pivot[j]) - (fac * pivot[j][k : k + 1, :]) * inv
                    )
            pivot = fresh
            gain = jnp.where(ri == k, root, 1.0)
            for j in range(k + 1):
                x[j] = (x[j] - under * x[j][k : k + 1, :]) * gain
        z = tree([pivot[j] * q1[j : j + 1, :] for j in range(b)])
        if more:
            pivot_next = []
            for c in range(b):
                part = tree([pivot[j] * ahead[c][j : j + 1, :] for j in range(b)])
                pivot_next.append(
                    below_new[c] - tree([below_old[k] * part[k : k + 1, :] for k in range(b)])
                )
        z_rows = [jnp.broadcast_to(z[j : j + 1, :], (b, n)) for j in range(b)]
        for i in range(p + 1, n // b):
            src = rows[i]
            rows[i] = jnp.where(inside, 0.0, src) - tree(
                [lane(src, b * p + j) * z_rows[j] for j in range(b)]
            )
        upper = tree([x[j] * q[j : j + 1, :] for j in range(b)])
        inverse = tree([x[j] * q1[j : j + 1, :] for j in range(b)])
        diag = ci - b * p >= ri
        uppers.append(jnp.where(diag, upper, 0.0))
        inverses.append(jnp.where(ci - b * p <= ri, inverse, 0.0))
        if more:
            pivot = pivot_next
        for _ in range(-(-len(beside) // (n // b - p))):
            beside.pop(0)()
    return jnp.concatenate(uppers, axis=0), jnp.concatenate(inverses, axis=0)


def factor_kernel(scale, g_ref, t_hbm, o_hbm, r_ref, rows, w_ref, stage, in_sem, out_sem):
    load = pltpu.make_async_copy(t_hbm, rows, in_sem)
    load.start()
    b, n = 128, 4
    chunk = PIECE
    pieces = rows.shape[0] // chunk
    g, r, w, held, outs = {}, {}, {}, {}, []
    at = 0
    for i in range(n):
        for j in range(i, n):
            g[i, j] = g_ref[at]
            at += 1

    def spot(i, j):
        return slice(i * b, (i + 1) * b), slice(j * b, (j + 1) * b)

    def row_of(p, j):
        r[p, j] = exact(w[p, p], g[p, j], NN)

    def update(p, i, j):
        g[i, j] = g[i, j] - exact(r[p, i], r[p, j], TN)

    def hold(i, j):
        held[i, j] = tree([exact(r[k, i], w[k, j], TN) for k in range(j, i)])

    def store_w(i, j):
        value = w[i, j] * scale
        high = value.astype(jnp.bfloat16)
        low = (value - high.astype(jnp.float32)).astype(jnp.bfloat16)
        w_ref[2 * i * b : (2 * i + 1) * b, spot(i, j)[1]] = high
        w_ref[(2 * i + 1) * b : (2 * i + 2) * b, spot(i, j)[1]] = low

    def finish_row(p):
        if p:
            behind = exact(w[p, p], jnp.concatenate([held[p, j] for j in range(p)], axis=1), NN)
            for j in range(p):
                w[p, j] = -behind[:, j * b : (j + 1) * b]
        for j in range(p + 1):
            store_w(p, j)

    def store_r(p):
        for j in range(n):
            r_ref[spot(p, j)] = r[p, j] * (1.0 / scale) if j >= p else jnp.zeros((b, b), jnp.float32)

    def basis_piece(p, at):
        end = (p + 1) * b
        here = slice(at * chunk, (at + 1) * chunk)
        both = lax.dot_general(
            w_ref[2 * p * b : (2 * p + 2) * b, :end],
            rows[here, :end],
            NT,
            preferred_element_type=jnp.float32,
        )
        stage[p, :, here] = (both[:b] + both[b:]).astype(jnp.bfloat16)

    def send_row(p):
        item = pltpu.make_async_copy(stage.at[p], o_hbm.at[pl.ds(p * b, b), :], out_sem.at[p])
        item.start()
        outs.append(item)

    beside = []
    for p in range(n):
        r[p, p], w[p, p] = eliminate(g[p, p], beside)
        assert not beside
        if p == 0:
            load.wait()
        else:
            send_row(p - 1)
        if p + 1 < n:
            row_of(p, p + 1)
            update(p, p + 1, p + 1)
            for j in range(p + 2, n):
                beside.append(functools.partial(row_of, p, j))
                for i in range(p + 1, j + 1):
                    beside.append(functools.partial(update, p, i, j))
            beside.append(functools.partial(finish_row, p))
            for j in range(p + 1):
                beside.append(functools.partial(hold, p + 1, j))
            beside.append(functools.partial(store_r, p))
            for at in range(pieces):
                beside.append(functools.partial(basis_piece, p, at))
        else:
            finish_row(p)
            store_r(p)
            for at in range(pieces):
                basis_piece(p, at)
            send_row(p)
    for item in outs:
        item.wait()


def shards(n_lat, n_lon, velocity, lon_metric, lat_metric, wet_index, wet_count):
    days, nx, ny = velocity.shape[1:]
    cols = 2 * days
    cells = nx * ny
    f32, bf16 = jnp.float32, jnp.bfloat16
    shape = jax.ShapeDtypeStruct
    params = pltpu.CompilerParams(vmem_limit_bytes=BIG)

    dma = pltpu.SemaphoreType.DMA
    lane, group = 128, 16
    f, gram = pl.pallas_call(
        functools.partial(field_kernel, n_lat, n_lon),
        in_specs=[VMEM, SMEM, VMEM, VMEM, ANY],
        out_specs=[ANY, VMEM],
        out_shape=[shape((cells, cols), bf16), shape((10, 128, 128), f32)],
        scratch_shapes=[
            pltpu.VMEM((2, lane, nx, ny), bf16),
            pltpu.VMEM((lane, nx, ny), f32),
            pltpu.VMEM((nx + 2, ny, cols), bf16),
            pltpu.VMEM((cells, cols), bf16),
            pltpu.VMEM((nx // group, ny, group), f32),
            pltpu.VMEM((nx // group, ny, group), f32),
            pltpu.VMEM((cols, cols), f32),
            pltpu.VMEM((2, nx, lane), f32),
            pltpu.VMEM((2, 4, nx, lane), bf16),
            pltpu.VMEM((2, 4, nx, lane), bf16),
            pltpu.VMEM((4, nx, lane), f32),
            pltpu.VMEM((4, nx, lane), f32),
            dma((2,)),
            dma((3,)),
            dma((4, 4)),
            dma((4, 4)),
        ],
        compiler_params=pltpu.CompilerParams(
            collective_id=0, has_side_effects=True, vmem_limit_bytes=BIG
        ),
    )(
        wet_index.reshape(nx, ny), wet_count, lon_metric, lat_metric, velocity.reshape(cols, nx, ny)
    )

    total, picked = pl.pallas_call(
        sum_kernel,
        in_specs=[SMEM, VMEM, ANY],
        out_specs=[VMEM, ANY],
        out_shape=[shape((2, 16, 40, 128), f32), shape((cells, cols), bf16)],
        scratch_shapes=[
            pltpu.VMEM((cells, cols), bf16),
            pltpu.VMEM((cells, 4, cols // 4), f32),
            pltpu.VMEM((cells, 4, cols // 4), f32),
            pltpu.VMEM((16, 40, 128), f32),
            pltpu.VMEM((16, 40, 128), f32),
            pltpu.VMEM((16, 40, 128), f32),
            pltpu.VMEM((8, 40, 128), f32),
            pltpu.VMEM((2, 40, 128), f32),
            pltpu.VMEM((16, 40, 128), f32),
            *[dma((n,)) for n in (1, 1, 15, 15, 7, 7, 15, 15, 1, 1)],
            dma(()),
            dma((4,)),
        ],
        compiler_params=pltpu.CompilerParams(
            collective_id=1, has_side_effects=True, vmem_limit_bytes=BIG
        ),
    )(wet_index, gram.reshape(2, 16, 40, 128), f)

    scale = math.sqrt(cells * n_lat * n_lon)
    basis, r_factor = pl.pallas_call(
        functools.partial(factor_kernel, scale),
        in_specs=[VMEM, ANY],
        out_specs=[ANY, VMEM],
        out_shape=[shape((cols, cells), bf16), shape((cols, cols), f32)],
        scratch_shapes=[
            pltpu.VMEM((cells, cols), bf16),
            pltpu.VMEM((2 * cols, cols), bf16),
            pltpu.VMEM((4, 128, cells), bf16),
            dma(()),
            dma((4,)),
        ],
        compiler_params=params,
    )(total.reshape(10, 128, 128), picked)
    return basis, r_factor


def solution(mesh):
    n_lat, n_lon = mesh.shape["lat"], mesh.shape["lon"]
    placed = (
        P(None, None, "lon", "lat"),
        P("lon", "lat"),
        P("lon", "lat"),
        P(("lat", "lon")),
        P(("lat", "lon")),
    )
    return jax.shard_map(
        functools.partial(shards, n_lat, n_lon),
        mesh=mesh,
        in_specs=placed,
        out_specs=(P(None, ("lat", "lon")), P()),
        check_vma=False,
    )
```

```python
import functools
import math

import jax
import jax.numpy as jnp
from jax import lax
from jax.experimental import pallas as pl
from jax.experimental.pallas import tpu as pltpu
from jax.sharding import PartitionSpec as P

MESH = pl.DeviceIdType.MESH
VMEM = pl.BlockSpec(memory_space=pltpu.VMEM)
SMEM = pl.BlockSpec(memory_space=pltpu.SMEM)
ANY = pl.BlockSpec(memory_space=pl.ANY)
BIG = 60 << 20
PIECE = 1536
NT = (((1,), (1,)), ((), ()))
TN = (((0,), (0,)), ((), ()))
NN = (((1,), (0,)), ((), ()))


def field_kernel(
    n_lat, n_lon, order, idx, count, lon_ref, lat_ref, v_hbm, out, t_hbm,
    vin, wide, vt, f, lon_t, lat_t, acc, edge, edge16, from16, south, north,
    spread, picked, g, r0, s0, r1, r2, s1, r3,
    load_sem, store_sem, send, recv,
    send0, recv0, send1, recv1, send2, recv2, send3, recv3, send4, recv4,
):
    lat, lon = lax.axis_index("lat"), lax.axis_index("lon")
    nx, ny = lon_ref.shape
    lane = vin.shape[1]
    top = lat // (n_lat - 1)
    is_top = lat == n_lat - 1
    right = (lat, lax.rem(lon + 1, n_lon))
    left = (lat, lax.rem(lon + n_lon - 1, n_lon))
    up = (lat + 1 - top, lon + top * (n_lon - 1 - 2 * lon))
    down = (jnp.where(lat == 0, lat, lat - 1), lon)

    def load(step):
        c = lax.rem(step, 2) * 2 + step // 2
        return pltpu.make_async_copy(
            v_hbm.at[pl.ds(c * lane, lane)], vin.at[lax.rem(step, 2)], load_sem.at[lax.rem(step, 2)]
        )

    core, cx = lax.rem(lat, 2), lat // 2
    cy, cz = lon // 8, lax.rem(lon, 8)
    mine = cx * 4 + cy
    mate = (lat + 1 - 2 * core, lon)

    def plane(off):
        spot = lax.rem(mine + off, 16)
        return spot, (2 * (spot // 4) + core, 8 * lax.rem(spot, 4) + cz)

    def along_z(off):
        return (lat, 8 * cy + lax.rem(cz + off, 8))

    load(0).start()
    barrier = pltpu.get_barrier_semaphore()
    others = [right, left, up, mate]
    others += [plane(off)[1] for off in range(1, 16)] + [along_z(off) for off in range(1, 8)]
    for other in others:
        pl.semaphore_signal(barrier, inc=1, device_id=other, device_id_type=MESH)

    @pl.when(lat > 0)
    def _():
        pl.semaphore_signal(barrier, inc=1, device_id=down, device_id_type=MESH)

    live = count[0]
    total = jnp.zeros((nx, ny), jnp.float32)
    width = 8 * ny
    for at in range(nx // 8):
        cell = jnp.concatenate([idx[8 * at + i : 8 * at + i + 1, :] for i in range(8)], axis=1)
        place = lax.broadcasted_iota(jnp.int32, (1, width), 1) + at * width
        column = jnp.where(place < live, cell // ny, -1)
        hot_x = lax.broadcasted_iota(jnp.int32, (nx, width), 0) == column
        hot_y = lax.broadcasted_iota(jnp.int32, (ny, width), 0) == cell % ny
        total += lax.dot_general(
            hot_x.astype(jnp.float32).astype(jnp.bfloat16),
            hot_y.astype(jnp.float32).astype(jnp.bfloat16),
            NT,
            preferred_element_type=jnp.float32,
        )
    lon_m = 0.5 * lon_ref[...] * total
    lat_m = 0.5 * lat_ref[...] * total
    group = lon_t.shape[2]
    for at in range(nx // group):
        lon_t[at] = lon_m[at * group : (at + 1) * group].T
        lat_t[at] = lat_m[at * group : (at + 1) * group].T
    pl.semaphore_wait(barrier, jnp.where(lat > 0, 27, 26))

    def copy(src, dst, c, out, into, to):
        return pltpu.make_async_remote_copy(
            src_ref=src,
            dst_ref=dst,
            send_sem=send.at[c, out],
            recv_sem=recv.at[c, into],
            device_id=to,
            device_id_type=MESH,
        )

    def lanes(c):
        return pl.ds(pl.multiple_of(c * lane, lane), lane)

    def to_right(c):
        return copy(vt.at[nx, :, lanes(c)], vt.at[0, :, lanes(c)], c, 0, 0, right)

    def to_left(c):
        return copy(vt.at[1, :, lanes(c)], vt.at[nx + 1, :, lanes(c)], c, 1, 1, left)

    def to_up(c):
        return copy(edge16.at[1, c], from16.at[0, c], c, 2, 2, up)

    def to_fold(c):
        return copy(edge16.at[1, c], from16.at[1, c], c, 2, 3, up)

    def to_down(c):
        return copy(edge16.at[0, c], from16.at[1, c], c, 3, 3, down)

    def turn(step, _):
        c = lax.rem(step, 2) * 2 + step // 2
        load(step).wait()

        @pl.when(step < 3)
        def _():
            load(step + 1).start()

        wide[...] = vin[lax.rem(step, 2)].astype(jnp.float32)
        for x in range(nx):
            turned = wide[:, x, :].T
            vt[x + 1, :, lanes(c)] = turned.astype(jnp.bfloat16)
            edge[0, x : x + 1, :] = turned[:1, :]
            edge[1, x : x + 1, :] = turned[-1:, :]
        edge16[0, c] = edge[0].astype(jnp.bfloat16)
        edge16[1, c] = edge[1].astype(jnp.bfloat16)

        @pl.when(is_top)
        def _():
            to_fold(c).start()

        @pl.when(jnp.logical_not(is_top))
        def _():
            to_up(c).start()

        @pl.when(lat > 0)
        def _():
            to_down(c).start()

        to_right(c).start()
        to_left(c).start()
        return 0

    lax.fori_loop(0, 4, turn, 0)

    row = lax.broadcasted_iota(jnp.int32, (ny, 1), 0)
    iy = lax.broadcasted_iota(jnp.int32, (ny, ny), 0)
    ix = lax.broadcasted_iota(jnp.int32, (ny, ny), 1)
    band = (ix == iy + 1).astype(jnp.float32) - (ix == iy - 1).astype(jnp.float32)
    band = band.astype(jnp.bfloat16)
    acc[...] = jnp.zeros_like(acc)

    for h in range(2):
        for c in (h, 2 + h):
            to_right(c).wait_recv()
            to_left(c).wait_recv()
            to_fold(c).wait_recv()
            arrived = from16[1, c].astype(jnp.float32)
            north[c] = jnp.where(is_top, -arrived, arrived)

            @pl.when(lat == 0)
            def _():
                south[c] = jnp.zeros((nx, lane), jnp.float32)

            @pl.when(lat > 0)
            def _():
                to_up(c).wait_recv()
                south[c] = from16[0, c].astype(jnp.float32)

        cu, cv = h, 2 + h
        lu, lv = slice(cu * lane, cu * lane + lane), slice(cv * lane, cv * lane + lane)

        def fields(at_group, _):
            m_lon, m_lat = lon_t[at_group], lat_t[at_group]
            for at in range(group):
                x = at_group * group + at
                x_top = x + top * (nx - 1 - 2 * x)
                here = pl.ds(pl.multiple_of(x * ny, ny), ny)
                a, b = m_lon[:, at : at + 1], m_lat[:, at : at + 1]
                u_x = vt[x + 2, :, lu].astype(jnp.float32) - vt[x, :, lu].astype(jnp.float32)
                v_x = vt[x + 2, :, lv].astype(jnp.float32) - vt[x, :, lv].astype(jnp.float32)

                def over_y(c, where):
                    inner = lax.dot_general(
                        band, vt[x + 1, :, where], NN, preferred_element_type=jnp.float32
                    )
                    inner = inner + jnp.where(row == ny - 1, north[c, pl.ds(x_top, 1), :], 0.0)
                    return inner - jnp.where(row == 0, south[c, pl.ds(x, 1), :], 0.0)

                f[here, lu] = (a * v_x - b * over_y(cu, lu)).astype(jnp.bfloat16)
                f[here, lv] = (a * u_x + b * over_y(cv, lv)).astype(jnp.bfloat16)
            if h == 1:
                span = pl.ds(pl.multiple_of(at_group * (group * ny), group * ny), group * ny)
                acc[...] += lax.dot_general(
                    f[span, :], f[span, :], TN, preferred_element_type=jnp.float32
                )
            return 0

        lax.fori_loop(0, nx // group, fields, 0)
    tile = 0
    for i in range(4):
        for j in range(i, 4):
            for k in range(16):
                half, spot, low = tile // 80, tile % 80 // 5, tile % 5 * 8
                g[half, spot, low : low + 8, :] = acc[
                    i * 128 + k * 8 : i * 128 + k * 8 + 8, j * 128 : (j + 1) * 128
                ]
                tile += 1
    cells, cols = f.shape
    spans = (pl.ds(0, 24), pl.ds(24, 16))
    started = []

    def widen(at, _):
        here = pl.ds(pl.multiple_of(at * 128, 128), 128)
        spread[here] = f[here, :].astype(jnp.float32).reshape(128, 4, cols // 4)
        return 0

    def pick(at, _):
        base = at * 64
        taken = [spread[order[base + u]] for u in range(64)]
        for u in range(64):
            picked[base + u] = taken[u]
        return 0

    def pick_part(low, high):
        lax.fori_loop(low * 8, high * 8, pick, 0)

    def narrow(at, _):
        here = pl.ds(pl.multiple_of(at * 128, 128), 128)
        f[here, :] = picked[here].reshape(128, cols).astype(jnp.bfloat16)
        return 0

    def go(src, dst, out_sem, in_sem, to):
        item = pltpu.make_async_remote_copy(
            src_ref=src,
            dst_ref=dst,
            send_sem=out_sem,
            recv_sem=in_sem,
            device_id=to,
            device_id_type=MESH,
        )
        item.start()
        started.append(item)
        return item

    def pair_start(k):
        span = spans[k]
        return go(g.at[1 - core, :, span], r0.at[:, span], send0.at[k], recv0.at[k], mate)

    def gather_start(k, item):
        span = spans[k]
        item.wait_recv()
        s0[:, span] = g[core, :, span] + r0[:, span]
        items = []
        for off in range(1, 16):
            spot, to = plane(off)
            items.append(
                go(
                    s0.at[spot, span],
                    r1.at[mine, span],
                    send1.at[k, off - 1],
                    recv1.at[k, off - 1],
                    to,
                )
            )
        r1[mine, span] = s0[mine, span]
        return items

    def column_start(k, items):
        span = spans[k]
        for item in items:
            item.wait_recv()
        total = r1[0, span]
        for at in range(1, 16):
            total = total + r1[at, span]
        s1[0, span] = total
        r2[cz, span] = total
        return [
            go(
                s1.at[0, span],
                r2.at[cz, span],
                send2.at[k, off - 1],
                recv2.at[k, off - 1],
                along_z(off),
            )
            for off in range(1, 8)
        ]

    def back_start(k, items):
        span = spans[k]
        for item in items:
            item.wait_recv()
        total = r2[0, span]
        for at in range(1, 8):
            total = total + r2[at, span]
        s1[1, span] = total
        r3[mine, span] = total
        return [
            go(
                s1.at[1, span],
                r3.at[mine, span],
                send3.at[k, off - 1],
                recv3.at[k, off - 1],
                plane(off)[1],
            )
            for off in range(1, 16)
        ]

    def last_start(k, items):
        span = spans[k]
        for item in items:
            item.wait_recv()
        return go(r3.at[:, span], out.at[core, :, span], send4.at[k], recv4.at[k], mate)

    pairs = [pair_start(k) for k in range(2)]
    lax.fori_loop(0, cells // 128, widen, 0)
    planes = [gather_start(k, pairs[k]) for k in range(2)]
    pick_part(0, 4)
    first = column_start(0, planes[0])
    pick_part(4, 5)
    columns = [first, column_start(1, planes[1])]
    pick_part(5, 8)
    first = back_start(0, columns[0])
    pick_part(8, 9)
    backs = [first, back_start(1, columns[1])]
    pick_part(9, 12)
    lax.fori_loop(0, cells // 128, narrow, 0)
    store = pltpu.make_async_copy(f, t_hbm, store_sem)
    store.start()
    lasts = [last_start(k, backs[k]) for k in range(2)]
    out[core] = r3[...]
    for item in lasts:
        item.wait_recv()
    store.wait()
    for item in started:
        item.wait_send()
    for c in range(4):
        to_right(c).wait_send()
        to_left(c).wait_send()

        @pl.when(is_top)
        def _():
            to_fold(c).wait_send()

        @pl.when(jnp.logical_not(is_top))
        def _():
            to_up(c).wait_send()

        @pl.when(lat > 0)
        def _():
            to_down(c).wait_send()


def exact(a, b, dims):
    return lax.dot_general(
        a, b, dims, precision=lax.Precision.HIGHEST, preferred_element_type=jnp.float32
    )


def tree(terms):
    while len(terms) > 1:
        odd = terms[-1:] if len(terms) % 2 else []
        terms = [p + q for p, q in zip(terms[0::2], terms[1::2])] + odd
    return terms[0]


def eliminate(a, beside):
    n = a.shape[0]
    b = 8
    rows = [a[b * i : b * i + b, :] for i in range(n // b)]
    ci = lax.broadcasted_iota(jnp.int32, (b, n), 1)
    ri = lax.broadcasted_iota(jnp.int32, (b, n), 0)
    unit = [jnp.where(ri == j, 1.0, 0.0) for j in range(b)]

    def lane(v, c):
        return jnp.broadcast_to(v[:, c : c + 1], (b, n))

    pivot = [lane(rows[0], j) for j in range(b)]
    uppers, inverses = [], []
    for p in range(n // b):
        q = rows[p]
        x = list(unit)
        inside = (ci >= b * p) & (ci < b * p + b)
        q1 = jnp.where(inside, jnp.where(ci - b * p == ri, 1.0, 0.0), q)
        more = p + 1 < n // b
        if more:
            below = rows[p + 1]
            below_old = [lane(below, b * p + j) for j in range(b)]
            below_new = [lane(below, b * p + b + j) for j in range(b)]
            ahead = [lane(q, b * p + b + j) for j in range(b)]
        for k in range(b):
            value = jnp.broadcast_to(pivot[k][k : k + 1, :], (b, n))
            inv = 1.0 / value
            root = lax.rsqrt(value)
            col = jnp.where(ri == k, 0.0, pivot[k])
            fac = jnp.where(ri == k, -1.0, pivot[k])
            col_inv = col * inv
            under = jnp.where(ri > k, col_inv, 0.0)
            fresh = []
            for j in range(b):
                if j == k:
                    fresh.append(jnp.where(ri == k, inv, -col_inv))
                else:
                    fresh.append(
                        jnp.where(ri == k, 0.0, pivot[j]) - (fac * pivot[j][k : k + 1, :]) * inv
                    )
            pivot = fresh
            gain = jnp.where(ri == k, root, 1.0)
            for j in range(k + 1):
                x[j] = (x[j] - under * x[j][k : k + 1, :]) * gain
        z = tree([pivot[j] * q1[j : j + 1, :] for j in range(b)])
        if more:
            pivot_next = []
            for c in range(b):
                part = tree([pivot[j] * ahead[c][j : j + 1, :] for j in range(b)])
                pivot_next.append(
                    below_new[c] - tree([below_old[k] * part[k : k + 1, :] for k in range(b)])
                )
        z_rows = [jnp.broadcast_to(z[j : j + 1, :], (b, n)) for j in range(b)]
        for i in range(p + 1, n // b):
            src = rows[i]
            rows[i] = jnp.where(inside, 0.0, src) - tree(
                [lane(src, b * p + j) * z_rows[j] for j in range(b)]
            )
        upper = tree([x[j] * q[j : j + 1, :] for j in range(b)])
        inverse = tree([x[j] * q1[j : j + 1, :] for j in range(b)])
        diag = ci - b * p >= ri
        uppers.append(jnp.where(diag, upper, 0.0))
        inverses.append(jnp.where(ci - b * p <= ri, inverse, 0.0))
        if more:
            pivot = pivot_next
        for _ in range(-(-len(beside) // (n // b - p))):
            beside.pop(0)()
    return jnp.concatenate(uppers, axis=0), jnp.concatenate(inverses, axis=0)


def factor_kernel(scale, g_ref, t_hbm, o_hbm, r_ref, rows, w_ref, stage, in_sem, out_sem):
    load = pltpu.make_async_copy(t_hbm, rows, in_sem)
    load.start()
    b, n = 128, 4
    chunk = PIECE
    pieces = rows.shape[0] // chunk
    g, r, w, held, outs = {}, {}, {}, {}, []
    at = 0
    for i in range(n):
        for j in range(i, n):
            g[i, j] = g_ref[at]
            at += 1

    def spot(i, j):
        return slice(i * b, (i + 1) * b), slice(j * b, (j + 1) * b)

    def row_of(p, j):
        r[p, j] = exact(w[p, p], g[p, j], NN)

    def update(p, i, j):
        g[i, j] = g[i, j] - exact(r[p, i], r[p, j], TN)

    def hold(i, j):
        held[i, j] = tree([exact(r[k, i], w[k, j], TN) for k in range(j, i)])

    def store_w(i, j):
        value = w[i, j] * scale
        high = value.astype(jnp.bfloat16)
        low = (value - high.astype(jnp.float32)).astype(jnp.bfloat16)
        w_ref[2 * i * b : (2 * i + 1) * b, spot(i, j)[1]] = high
        w_ref[(2 * i + 1) * b : (2 * i + 2) * b, spot(i, j)[1]] = low

    def finish_row(p):
        if p:
            behind = exact(w[p, p], jnp.concatenate([held[p, j] for j in range(p)], axis=1), NN)
            for j in range(p):
                w[p, j] = -behind[:, j * b : (j + 1) * b]
        for j in range(p + 1):
            store_w(p, j)

    def store_r(p):
        for j in range(n):
            r_ref[spot(p, j)] = r[p, j] * (1.0 / scale) if j >= p else jnp.zeros((b, b), jnp.float32)

    def basis_piece(p, at):
        end = (p + 1) * b
        here = slice(at * chunk, (at + 1) * chunk)
        both = lax.dot_general(
            w_ref[2 * p * b : (2 * p + 2) * b, :end],
            rows[here, :end],
            NT,
            preferred_element_type=jnp.float32,
        )
        stage[p, :, here] = (both[:b] + both[b:]).astype(jnp.bfloat16)

    def send_row(p):
        item = pltpu.make_async_copy(stage.at[p], o_hbm.at[pl.ds(p * b, b), :], out_sem.at[p])
        item.start()
        outs.append(item)

    beside = []
    for p in range(n):
        r[p, p], w[p, p] = eliminate(g[p, p], beside)
        assert not beside
        if p == 0:
            load.wait()
        else:
            send_row(p - 1)
        if p + 1 < n:
            row_of(p, p + 1)
            update(p, p + 1, p + 1)
            for j in range(p + 2, n):
                beside.append(functools.partial(row_of, p, j))
                for i in range(p + 1, j + 1):
                    beside.append(functools.partial(update, p, i, j))
            beside.append(functools.partial(finish_row, p))
            for j in range(p + 1):
                beside.append(functools.partial(hold, p + 1, j))
            beside.append(functools.partial(store_r, p))
            for at in range(pieces):
                beside.append(functools.partial(basis_piece, p, at))
        else:
            finish_row(p)
            store_r(p)
            for at in range(pieces):
                basis_piece(p, at)
            send_row(p)
    for item in outs:
        item.wait()


def shards(n_lat, n_lon, velocity, lon_metric, lat_metric, wet_index, wet_count):
    days, nx, ny = velocity.shape[1:]
    cols = 2 * days
    cells = nx * ny
    f32, bf16 = jnp.float32, jnp.bfloat16
    shape = jax.ShapeDtypeStruct
    params = pltpu.CompilerParams(vmem_limit_bytes=BIG)

    dma = pltpu.SemaphoreType.DMA
    lane, group = 128, 16
    total, picked = pl.pallas_call(
        functools.partial(field_kernel, n_lat, n_lon),
        in_specs=[SMEM, VMEM, SMEM, VMEM, VMEM, ANY],
        out_specs=[VMEM, ANY],
        out_shape=[shape((2, 16, 40, 128), f32), shape((cells, cols), bf16)],
        scratch_shapes=[
            pltpu.VMEM((2, lane, nx, ny), bf16),
            pltpu.VMEM((lane, nx, ny), f32),
            pltpu.VMEM((nx + 2, ny, cols), bf16),
            pltpu.VMEM((cells, cols), bf16),
            pltpu.VMEM((nx // group, ny, group), f32),
            pltpu.VMEM((nx // group, ny, group), f32),
            pltpu.VMEM((cols, cols), f32),
            pltpu.VMEM((2, nx, lane), f32),
            pltpu.VMEM((2, 4, nx, lane), bf16),
            pltpu.VMEM((2, 4, nx, lane), bf16),
            pltpu.VMEM((4, nx, lane), f32),
            pltpu.VMEM((4, nx, lane), f32),
            pltpu.VMEM((cells, 4, cols // 4), f32),
            pltpu.VMEM((cells, 4, cols // 4), f32),
            pltpu.VMEM((2, 16, 40, 128), f32),
            pltpu.VMEM((16, 40, 128), f32),
            pltpu.VMEM((16, 40, 128), f32),
            pltpu.VMEM((16, 40, 128), f32),
            pltpu.VMEM((8, 40, 128), f32),
            pltpu.VMEM((2, 40, 128), f32),
            pltpu.VMEM((16, 40, 128), f32),
            dma((2,)),
            dma(()),
            dma((4, 4)),
            dma((4, 4)),
            *[dma((2,) + n) for n in ((), (), (15,), (15,), (7,), (7,), (15,), (15,), (), ())],
        ],
        compiler_params=pltpu.CompilerParams(
            collective_id=0, has_side_effects=True, vmem_limit_bytes=BIG
        ),
    )(
        wet_index,
        wet_index.reshape(nx, ny),
        wet_count,
        lon_metric,
        lat_metric,
        velocity.reshape(cols, nx, ny),
    )

    scale = math.sqrt(cells * n_lat * n_lon)
    basis, r_factor = pl.pallas_call(
        functools.partial(factor_kernel, scale),
        in_specs=[VMEM, ANY],
        out_specs=[ANY, VMEM],
        out_shape=[shape((cols, cells), bf16), shape((cols, cols), f32)],
        scratch_shapes=[
            pltpu.VMEM((cells, cols), bf16),
            pltpu.VMEM((2 * cols, cols), bf16),
            pltpu.VMEM((4, 128, cells), bf16),
            dma(()),
            dma((4,)),
        ],
        compiler_params=params,
    )(total.reshape(10, 128, 128), picked)
    return basis, r_factor


def solution(mesh):
    n_lat, n_lon = mesh.shape["lat"], mesh.shape["lon"]
    placed = (
        P(None, None, "lon", "lat"),
        P("lon", "lat"),
        P("lon", "lat"),
        P(("lat", "lon")),
        P(("lat", "lon")),
    )
    return jax.shard_map(
        functools.partial(shards, n_lat, n_lon),
        mesh=mesh,
        in_specs=placed,
        out_specs=(P(None, ("lat", "lon")), P()),
        check_vma=False,
    )
```

```python
import functools
import math

import jax
import jax.numpy as jnp
from jax import lax
from jax.experimental import pallas as pl
from jax.experimental.pallas import tpu as pltpu
from jax.sharding import PartitionSpec as P

MESH = pl.DeviceIdType.MESH
VMEM = pl.BlockSpec(memory_space=pltpu.VMEM)
SMEM = pl.BlockSpec(memory_space=pltpu.SMEM)
ANY = pl.BlockSpec(memory_space=pl.ANY)
BIG = 60 << 20
PIECE = 1536
NT = (((1,), (1,)), ((), ()))
TN = (((0,), (0,)), ((), ()))
NN = (((1,), (0,)), ((), ()))


def field_kernel(
    n_lat, n_lon, order, idx, count, lon_ref, lat_ref, v_hbm, out, t_hbm,
    vin, wide, vt, f, lon_t, lat_t, acc, edge, edge16, from16, south, north,
    spread, picked, g, r0, s0, r1, r2, s1, r3,
    load_sem, store_sem, send, recv,
    send0, recv0, send1, recv1, send2, recv2, send3, recv3, send4, recv4,
):
    lat, lon = lax.axis_index("lat"), lax.axis_index("lon")
    nx, ny = lon_ref.shape
    lane = vin.shape[1]
    top = lat // (n_lat - 1)
    is_top = lat == n_lat - 1
    right = (lat, lax.rem(lon + 1, n_lon))
    left = (lat, lax.rem(lon + n_lon - 1, n_lon))
    up = (lat + 1 - top, lon + top * (n_lon - 1 - 2 * lon))
    down = (jnp.where(lat == 0, lat, lat - 1), lon)

    def load(step):
        c = lax.rem(step, 2) * 2 + step // 2
        return pltpu.make_async_copy(
            v_hbm.at[pl.ds(c * lane, lane)], vin.at[lax.rem(step, 2)], load_sem.at[lax.rem(step, 2)]
        )

    core, cx = lax.rem(lat, 2), lat // 2
    cy, cz = lon // 8, lax.rem(lon, 8)
    mine = cx * 4 + cy
    mate = (lat + 1 - 2 * core, lon)

    def plane(off):
        spot = lax.rem(mine + off, 16)
        return spot, (2 * (spot // 4) + core, 8 * lax.rem(spot, 4) + cz)

    def along_z(off):
        return (lat, 8 * cy + lax.rem(cz + off, 8))

    load(0).start()
    barrier = pltpu.get_barrier_semaphore()
    others = [right, left, up, mate]
    others += [plane(off)[1] for off in range(1, 16)] + [along_z(off) for off in range(1, 8)]
    for other in others:
        pl.semaphore_signal(barrier, inc=1, device_id=other, device_id_type=MESH)

    @pl.when(lat > 0)
    def _():
        pl.semaphore_signal(barrier, inc=1, device_id=down, device_id_type=MESH)

    live = count[0]
    total = jnp.zeros((nx, ny), jnp.float32)
    width = 8 * ny
    for at in range(nx // 8):
        cell = jnp.concatenate([idx[8 * at + i : 8 * at + i + 1, :] for i in range(8)], axis=1)
        place = lax.broadcasted_iota(jnp.int32, (1, width), 1) + at * width
        column = jnp.where(place < live, cell // ny, -1)
        hot_x = lax.broadcasted_iota(jnp.int32, (nx, width), 0) == column
        hot_y = lax.broadcasted_iota(jnp.int32, (ny, width), 0) == cell % ny
        total += lax.dot_general(
            hot_x.astype(jnp.float32).astype(jnp.bfloat16),
            hot_y.astype(jnp.float32).astype(jnp.bfloat16),
            NT,
            preferred_element_type=jnp.float32,
        )
    lon_m = 0.5 * lon_ref[...] * total
    lat_m = 0.5 * lat_ref[...] * total
    group = lon_t.shape[2]
    for at in range(nx // group):
        lon_t[at] = lon_m[at * group : (at + 1) * group].T
        lat_t[at] = lat_m[at * group : (at + 1) * group].T
    pl.semaphore_wait(barrier, jnp.where(lat > 0, 27, 26))

    def copy(src, dst, c, out, into, to):
        return pltpu.make_async_remote_copy(
            src_ref=src,
            dst_ref=dst,
            send_sem=send.at[c, out],
            recv_sem=recv.at[c, into],
            device_id=to,
            device_id_type=MESH,
        )

    def lanes(c):
        return pl.ds(pl.multiple_of(c * lane, lane), lane)

    def to_right(c):
        return copy(vt.at[nx, :, lanes(c)], vt.at[0, :, lanes(c)], c, 0, 0, right)

    def to_left(c):
        return copy(vt.at[1, :, lanes(c)], vt.at[nx + 1, :, lanes(c)], c, 1, 1, left)

    def to_up(c):
        return copy(edge16.at[1, c], from16.at[0, c], c, 2, 2, up)

    def to_fold(c):
        return copy(edge16.at[1, c], from16.at[1, c], c, 2, 3, up)

    def to_down(c):
        return copy(edge16.at[0, c], from16.at[1, c], c, 3, 3, down)

    def turn(step, _):
        c = lax.rem(step, 2) * 2 + step // 2
        load(step).wait()

        @pl.when(step < 3)
        def _():
            load(step + 1).start()

        wide[...] = vin[lax.rem(step, 2)].astype(jnp.float32)
        for x in range(nx):
            turned = wide[:, x, :].T
            vt[x + 1, :, lanes(c)] = turned.astype(jnp.bfloat16)
            edge[0, x : x + 1, :] = turned[:1, :]
            edge[1, x : x + 1, :] = turned[-1:, :]
        edge16[0, c] = edge[0].astype(jnp.bfloat16)
        edge16[1, c] = edge[1].astype(jnp.bfloat16)

        @pl.when(is_top)
        def _():
            to_fold(c).start()

        @pl.when(jnp.logical_not(is_top))
        def _():
            to_up(c).start()

        @pl.when(lat > 0)
        def _():
            to_down(c).start()

        to_right(c).start()
        to_left(c).start()
        return 0

    lax.fori_loop(0, 4, turn, 0)

    row = lax.broadcasted_iota(jnp.int32, (ny, 1), 0)
    iy = lax.broadcasted_iota(jnp.int32, (ny, ny), 0)
    ix = lax.broadcasted_iota(jnp.int32, (ny, ny), 1)
    band = (ix == iy + 1).astype(jnp.float32) - (ix == iy - 1).astype(jnp.float32)
    band = band.astype(jnp.bfloat16)
    acc[...] = jnp.zeros_like(acc)

    for h in range(2):
        for c in (h, 2 + h):
            to_right(c).wait_recv()
            to_left(c).wait_recv()
            to_fold(c).wait_recv()
            arrived = from16[1, c].astype(jnp.float32)
            north[c] = jnp.where(is_top, -arrived, arrived)

            @pl.when(lat == 0)
            def _():
                south[c] = jnp.zeros((nx, lane), jnp.float32)

            @pl.when(lat > 0)
            def _():
                to_up(c).wait_recv()
                south[c] = from16[0, c].astype(jnp.float32)

        cu, cv = h, 2 + h
        lu, lv = slice(cu * lane, cu * lane + lane), slice(cv * lane, cv * lane + lane)

        def fields(at_group, at, m_lon, m_lat):
            x = at_group * group + at
            x_top = x + top * (nx - 1 - 2 * x)
            here = pl.ds(x * ny if h else pl.multiple_of(x * ny, ny), ny)
            a, b = m_lon[:, at : at + 1], m_lat[:, at : at + 1]
            u_x = vt[x + 2, :, lu].astype(jnp.float32) - vt[x, :, lu].astype(jnp.float32)
            v_x = vt[x + 2, :, lv].astype(jnp.float32) - vt[x, :, lv].astype(jnp.float32)

            def over_y(c, where):
                inner = lax.dot_general(
                    band, vt[x + 1, :, where], NN, preferred_element_type=jnp.float32
                )
                inner = inner + jnp.where(row == ny - 1, north[c, pl.ds(x_top, 1), :], 0.0)
                return inner - jnp.where(row == 0, south[c, pl.ds(x, 1), :], 0.0)

            f[here, lu] = (a * v_x - b * over_y(cu, lu)).astype(jnp.bfloat16)
            f[here, lv] = (a * u_x + b * over_y(cv, lv)).astype(jnp.bfloat16)

        def multiply(at_group, low, high):
            span = pl.ds(at_group * group * ny, group * ny)
            acc[low:high, low:] += lax.dot_general(
                f[span, low:high], f[span, low:], TN, preferred_element_type=jnp.float32
            )

        def fields_of_group(at_group, _):
            m_lon, m_lat = lon_t[at_group], lat_t[at_group]
            for at in range(group):
                fields(at_group, at, m_lon, m_lat)
            return 0

        groups = nx // group
        middle = acc.shape[0] // 2
        if h == 0:
            lax.fori_loop(0, groups, fields_of_group, 0)
        else:
            for at_group in range(groups):
                m_lon, m_lat = lon_t[at_group], lat_t[at_group]
                for at in range(group):
                    fields(at_group, at, m_lon, m_lat)
                    if at_group and at == 3:
                        multiply(at_group - 1, 0, middle)
                    if at_group and at == 11:
                        multiply(at_group - 1, middle, 2 * middle)
            multiply(groups - 1, 0, middle)
            multiply(groups - 1, middle, 2 * middle)

    tile = 0
    for i in range(4):
        for j in range(i, 4):
            for k in range(16):
                half, spot, low = tile // 80, tile % 80 // 5, tile % 5 * 8
                g[half, spot, low : low + 8, :] = acc[
                    i * 128 + k * 8 : i * 128 + k * 8 + 8, j * 128 : (j + 1) * 128
                ]
                tile += 1
    cells, cols = f.shape
    spans = (pl.ds(0, 24), pl.ds(24, 16))
    started = []

    def widen(at, _):
        here = pl.ds(pl.multiple_of(at * 128, 128), 128)
        spread[here] = f[here, :].astype(jnp.float32).reshape(128, 4, cols // 4)
        return 0

    def pick(at, _):
        base = at * 64
        taken = [spread[order[base + u]] for u in range(64)]
        for u in range(64):
            picked[base + u] = taken[u]
        return 0

    def pick_part(low, high):
        lax.fori_loop(low * 8, high * 8, pick, 0)

    def narrow(at, _):
        here = pl.ds(pl.multiple_of(at * 128, 128), 128)
        f[here, :] = picked[here].reshape(128, cols).astype(jnp.bfloat16)
        return 0

    def go(src, dst, out_sem, in_sem, to):
        item = pltpu.make_async_remote_copy(
            src_ref=src,
            dst_ref=dst,
            send_sem=out_sem,
            recv_sem=in_sem,
            device_id=to,
            device_id_type=MESH,
        )
        item.start()
        started.append(item)
        return item

    def pair_start(k):
        span = spans[k]
        return go(g.at[1 - core, :, span], r0.at[:, span], send0.at[k], recv0.at[k], mate)

    def gather_start(k, item):
        span = spans[k]
        item.wait_recv()
        s0[:, span] = g[core, :, span] + r0[:, span]
        items = []
        for off in range(1, 16):
            spot, to = plane(off)
            items.append(
                go(
                    s0.at[spot, span],
                    r1.at[mine, span],
                    send1.at[k, off - 1],
                    recv1.at[k, off - 1],
                    to,
                )
            )
        r1[mine, span] = s0[mine, span]
        return items

    def column_start(k, items):
        span = spans[k]
        for item in items:
            item.wait_recv()
        total = r1[0, span]
        for at in range(1, 16):
            total = total + r1[at, span]
        s1[0, span] = total
        r2[cz, span] = total
        return [
            go(
                s1.at[0, span],
                r2.at[cz, span],
                send2.at[k, off - 1],
                recv2.at[k, off - 1],
                along_z(off),
            )
            for off in range(1, 8)
        ]

    def back_start(k, items):
        span = spans[k]
        for item in items:
            item.wait_recv()
        total = r2[0, span]
        for at in range(1, 8):
            total = total + r2[at, span]
        s1[1, span] = total
        r3[mine, span] = total
        return [
            go(
                s1.at[1, span],
                r3.at[mine, span],
                send3.at[k, off - 1],
                recv3.at[k, off - 1],
                plane(off)[1],
            )
            for off in range(1, 16)
        ]

    def last_start(k, items):
        span = spans[k]
        for item in items:
            item.wait_recv()
        return go(r3.at[:, span], out.at[core, :, span], send4.at[k], recv4.at[k], mate)

    pairs = [pair_start(k) for k in range(2)]
    lax.fori_loop(0, cells // 128, widen, 0)
    planes = [gather_start(k, pairs[k]) for k in range(2)]
    pick_part(0, 4)
    first = column_start(0, planes[0])
    pick_part(4, 5)
    columns = [first, column_start(1, planes[1])]
    pick_part(5, 8)
    first = back_start(0, columns[0])
    pick_part(8, 9)
    backs = [first, back_start(1, columns[1])]
    pick_part(9, 12)
    lax.fori_loop(0, cells // 128, narrow, 0)
    store = pltpu.make_async_copy(f, t_hbm, store_sem)
    store.start()
    lasts = [last_start(k, backs[k]) for k in range(2)]
    out[core] = r3[...]
    for item in lasts:
        item.wait_recv()
    store.wait()
    for item in started:
        item.wait_send()
    for c in range(4):
        to_right(c).wait_send()
        to_left(c).wait_send()

        @pl.when(is_top)
        def _():
            to_fold(c).wait_send()

        @pl.when(jnp.logical_not(is_top))
        def _():
            to_up(c).wait_send()

        @pl.when(lat > 0)
        def _():
            to_down(c).wait_send()


def exact(a, b, dims):
    return lax.dot_general(
        a, b, dims, precision=lax.Precision.HIGHEST, preferred_element_type=jnp.float32
    )


def tree(terms):
    while len(terms) > 1:
        odd = terms[-1:] if len(terms) % 2 else []
        terms = [p + q for p, q in zip(terms[0::2], terms[1::2])] + odd
    return terms[0]


def eliminate(a, beside):
    n = a.shape[0]
    b = 8
    rows = [a[b * i : b * i + b, :] for i in range(n // b)]
    ci = lax.broadcasted_iota(jnp.int32, (b, n), 1)
    ri = lax.broadcasted_iota(jnp.int32, (b, n), 0)
    unit = [jnp.where(ri == j, 1.0, 0.0) for j in range(b)]

    def lane(v, c):
        return jnp.broadcast_to(v[:, c : c + 1], (b, n))

    pivot = [lane(rows[0], j) for j in range(b)]
    uppers, inverses = [], []
    for p in range(n // b):
        q = rows[p]
        x = list(unit)
        inside = (ci >= b * p) & (ci < b * p + b)
        q1 = jnp.where(inside, jnp.where(ci - b * p == ri, 1.0, 0.0), q)
        more = p + 1 < n // b
        if more:
            below = rows[p + 1]
            below_old = [lane(below, b * p + j) for j in range(b)]
            below_new = [lane(below, b * p + b + j) for j in range(b)]
            ahead = [lane(q, b * p + b + j) for j in range(b)]
        for k in range(b):
            value = jnp.broadcast_to(pivot[k][k : k + 1, :], (b, n))
            inv = 1.0 / value
            root = lax.rsqrt(value)
            col = jnp.where(ri == k, 0.0, pivot[k])
            fac = jnp.where(ri == k, -1.0, pivot[k])
            col_inv = col * inv
            under = jnp.where(ri > k, col_inv, 0.0)
            fresh = []
            for j in range(b):
                if j == k:
                    fresh.append(jnp.where(ri == k, inv, -col_inv))
                else:
                    fresh.append(
                        jnp.where(ri == k, 0.0, pivot[j]) - (fac * pivot[j][k : k + 1, :]) * inv
                    )
            pivot = fresh
            gain = jnp.where(ri == k, root, 1.0)
            for j in range(k + 1):
                x[j] = (x[j] - under * x[j][k : k + 1, :]) * gain
        z = tree([pivot[j] * q1[j : j + 1, :] for j in range(b)])
        if more:
            pivot_next = []
            for c in range(b):
                part = tree([pivot[j] * ahead[c][j : j + 1, :] for j in range(b)])
                pivot_next.append(
                    below_new[c] - tree([below_old[k] * part[k : k + 1, :] for k in range(b)])
                )
        z_rows = [jnp.broadcast_to(z[j : j + 1, :], (b, n)) for j in range(b)]
        for i in range(p + 1, n // b):
            src = rows[i]
            rows[i] = jnp.where(inside, 0.0, src) - tree(
                [lane(src, b * p + j) * z_rows[j] for j in range(b)]
            )
        upper = tree([x[j] * q[j : j + 1, :] for j in range(b)])
        inverse = tree([x[j] * q1[j : j + 1, :] for j in range(b)])
        diag = ci - b * p >= ri
        uppers.append(jnp.where(diag, upper, 0.0))
        inverses.append(jnp.where(ci - b * p <= ri, inverse, 0.0))
        if more:
            pivot = pivot_next
        for _ in range(-(-len(beside) // (n // b - p))):
            beside.pop(0)()
    return jnp.concatenate(uppers, axis=0), jnp.concatenate(inverses, axis=0)


def factor_kernel(scale, g_ref, t_hbm, o_hbm, r_ref, rows, w_ref, stage, in_sem, out_sem):
    load = pltpu.make_async_copy(t_hbm, rows, in_sem)
    load.start()
    b, n = 128, 4
    chunk = PIECE
    pieces = rows.shape[0] // chunk
    g, r, w, held, outs = {}, {}, {}, {}, []
    at = 0
    for i in range(n):
        for j in range(i, n):
            g[i, j] = g_ref[at]
            at += 1

    def spot(i, j):
        return slice(i * b, (i + 1) * b), slice(j * b, (j + 1) * b)

    def row_of(p, j):
        r[p, j] = exact(w[p, p], g[p, j], NN)

    def update(p, i, j):
        g[i, j] = g[i, j] - exact(r[p, i], r[p, j], TN)

    def hold(i, j):
        held[i, j] = tree([exact(r[k, i], w[k, j], TN) for k in range(j, i)])

    def store_w(i, j):
        value = w[i, j] * scale
        high = value.astype(jnp.bfloat16)
        low = (value - high.astype(jnp.float32)).astype(jnp.bfloat16)
        w_ref[2 * i * b : (2 * i + 1) * b, spot(i, j)[1]] = high
        w_ref[(2 * i + 1) * b : (2 * i + 2) * b, spot(i, j)[1]] = low

    def finish_row(p):
        if p:
            behind = exact(w[p, p], jnp.concatenate([held[p, j] for j in range(p)], axis=1), NN)
            for j in range(p):
                w[p, j] = -behind[:, j * b : (j + 1) * b]
        for j in range(p + 1):
            store_w(p, j)

    def store_r(p):
        for j in range(n):
            r_ref[spot(p, j)] = r[p, j] * (1.0 / scale) if j >= p else jnp.zeros((b, b), jnp.float32)

    def basis_piece(p, at):
        end = (p + 1) * b
        here = slice(at * chunk, (at + 1) * chunk)
        both = lax.dot_general(
            w_ref[2 * p * b : (2 * p + 2) * b, :end],
            rows[here, :end],
            NT,
            preferred_element_type=jnp.float32,
        )
        stage[p, :, here] = (both[:b] + both[b:]).astype(jnp.bfloat16)

    def send_row(p):
        item = pltpu.make_async_copy(stage.at[p], o_hbm.at[pl.ds(p * b, b), :], out_sem.at[p])
        item.start()
        outs.append(item)

    beside = []
    for p in range(n):
        r[p, p], w[p, p] = eliminate(g[p, p], beside)
        assert not beside
        if p == 0:
            load.wait()
        else:
            send_row(p - 1)
        if p + 1 < n:
            row_of(p, p + 1)
            update(p, p + 1, p + 1)
            for j in range(p + 2, n):
                beside.append(functools.partial(row_of, p, j))
                for i in range(p + 1, j + 1):
                    beside.append(functools.partial(update, p, i, j))
            beside.append(functools.partial(finish_row, p))
            for j in range(p + 1):
                beside.append(functools.partial(hold, p + 1, j))
            beside.append(functools.partial(store_r, p))
            for at in range(pieces):
                beside.append(functools.partial(basis_piece, p, at))
        else:
            finish_row(p)
            store_r(p)
            for at in range(pieces):
                basis_piece(p, at)
            send_row(p)
    for item in outs:
        item.wait()


def shards(n_lat, n_lon, velocity, lon_metric, lat_metric, wet_index, wet_count):
    days, nx, ny = velocity.shape[1:]
    cols = 2 * days
    cells = nx * ny
    f32, bf16 = jnp.float32, jnp.bfloat16
    shape = jax.ShapeDtypeStruct
    params = pltpu.CompilerParams(vmem_limit_bytes=BIG)

    dma = pltpu.SemaphoreType.DMA
    lane, group = 128, 16
    total, picked = pl.pallas_call(
        functools.partial(field_kernel, n_lat, n_lon),
        in_specs=[SMEM, VMEM, SMEM, VMEM, VMEM, ANY],
        out_specs=[VMEM, ANY],
        out_shape=[shape((2, 16, 40, 128), f32), shape((cells, cols), bf16)],
        scratch_shapes=[
            pltpu.VMEM((2, lane, nx, ny), bf16),
            pltpu.VMEM((lane, nx, ny), f32),
            pltpu.VMEM((nx + 2, ny, cols), bf16),
            pltpu.VMEM((cells, cols), bf16),
            pltpu.VMEM((nx // group, ny, group), f32),
            pltpu.VMEM((nx // group, ny, group), f32),
            pltpu.VMEM((cols, cols), f32),
            pltpu.VMEM((2, nx, lane), f32),
            pltpu.VMEM((2, 4, nx, lane), bf16),
            pltpu.VMEM((2, 4, nx, lane), bf16),
            pltpu.VMEM((4, nx, lane), f32),
            pltpu.VMEM((4, nx, lane), f32),
            pltpu.VMEM((cells, 4, cols // 4), f32),
            pltpu.VMEM((cells, 4, cols // 4), f32),
            pltpu.VMEM((2, 16, 40, 128), f32),
            pltpu.VMEM((16, 40, 128), f32),
            pltpu.VMEM((16, 40, 128), f32),
            pltpu.VMEM((16, 40, 128), f32),
            pltpu.VMEM((8, 40, 128), f32),
            pltpu.VMEM((2, 40, 128), f32),
            pltpu.VMEM((16, 40, 128), f32),
            dma((2,)),
            dma(()),
            dma((4, 4)),
            dma((4, 4)),
            *[dma((2,) + n) for n in ((), (), (15,), (15,), (7,), (7,), (15,), (15,), (), ())],
        ],
        compiler_params=pltpu.CompilerParams(
            collective_id=0, has_side_effects=True, vmem_limit_bytes=BIG
        ),
    )(
        wet_index,
        wet_index.reshape(nx, ny),
        wet_count,
        lon_metric,
        lat_metric,
        velocity.reshape(cols, nx, ny),
    )

    scale = math.sqrt(cells * n_lat * n_lon)
    basis, r_factor = pl.pallas_call(
        functools.partial(factor_kernel, scale),
        in_specs=[VMEM, ANY],
        out_specs=[ANY, VMEM],
        out_shape=[shape((cols, cells), bf16), shape((cols, cols), f32)],
        scratch_shapes=[
            pltpu.VMEM((cells, cols), bf16),
            pltpu.VMEM((2 * cols, cols), bf16),
            pltpu.VMEM((4, 128, cells), bf16),
            dma(()),
            dma((4,)),
        ],
        compiler_params=params,
    )(total.reshape(10, 128, 128), picked)
    return basis, r_factor


def solution(mesh):
    n_lat, n_lon = mesh.shape["lat"], mesh.shape["lon"]
    placed = (
        P(None, None, "lon", "lat"),
        P("lon", "lat"),
        P("lon", "lat"),
        P(("lat", "lon")),
        P(("lat", "lon")),
    )
    return jax.shard_map(
        functools.partial(shards, n_lat, n_lon),
        mesh=mesh,
        in_specs=placed,
        out_specs=(P(None, ("lat", "lon")), P()),
        check_vma=False,
    )
```

```python
import functools
import math

import jax
import jax.numpy as jnp
from jax import lax
from jax.experimental import pallas as pl
from jax.experimental.pallas import tpu as pltpu
from jax.sharding import PartitionSpec as P

MESH = pl.DeviceIdType.MESH
VMEM = pl.BlockSpec(memory_space=pltpu.VMEM)
SMEM = pl.BlockSpec(memory_space=pltpu.SMEM)
ANY = pl.BlockSpec(memory_space=pl.ANY)
BIG = 60 << 20
PIECE = 1536
NT = (((1,), (1,)), ((), ()))
TN = (((0,), (0,)), ((), ()))
NN = (((1,), (0,)), ((), ()))


def field_kernel(
    n_lat, n_lon, order, idx, count, lon_ref, lat_ref, v_hbm, out, t_hbm,
    vin, wide, vt, f, lon_t, lat_t, acc, edge, edge16, from16, south, north,
    spread, picked, g, r0, s0, r1, r2, s1, r3,
    load_sem, store_sem, send, recv,
    send0, recv0, send1, recv1, send2, recv2, send3, recv3, send4, recv4,
):
    lat, lon = lax.axis_index("lat"), lax.axis_index("lon")
    nx, ny = lon_ref.shape
    lane = vin.shape[1]
    top = lat // (n_lat - 1)
    is_top = lat == n_lat - 1
    right = (lat, lax.rem(lon + 1, n_lon))
    left = (lat, lax.rem(lon + n_lon - 1, n_lon))
    up = (lat + 1 - top, lon + top * (n_lon - 1 - 2 * lon))
    down = (jnp.where(lat == 0, lat, lat - 1), lon)

    def load(step):
        c = lax.rem(step, 2) * 2 + step // 2
        return pltpu.make_async_copy(
            v_hbm.at[pl.ds(c * lane, lane)], vin.at[lax.rem(step, 2)], load_sem.at[lax.rem(step, 2)]
        )

    core, cx = lax.rem(lat, 2), lat // 2
    cy, cz = lon // 8, lax.rem(lon, 8)
    mine = cx * 4 + cy
    mate = (lat + 1 - 2 * core, lon)

    def plane(off):
        spot = lax.rem(mine + off, 16)
        return spot, (2 * (spot // 4) + core, 8 * lax.rem(spot, 4) + cz)

    def along_z(off):
        return (lat, 8 * cy + lax.rem(cz + off, 8))

    load(0).start()
    barrier = pltpu.get_barrier_semaphore()
    others = [right, left, up, mate]
    others += [plane(off)[1] for off in range(1, 16)] + [along_z(off) for off in range(1, 8)]
    for other in others:
        pl.semaphore_signal(barrier, inc=1, device_id=other, device_id_type=MESH)

    @pl.when(lat > 0)
    def _():
        pl.semaphore_signal(barrier, inc=1, device_id=down, device_id_type=MESH)

    live = count[0]
    total = jnp.zeros((nx, ny), jnp.float32)
    width = 8 * ny
    for at in range(nx // 8):
        cell = jnp.concatenate([idx[8 * at + i : 8 * at + i + 1, :] for i in range(8)], axis=1)
        place = lax.broadcasted_iota(jnp.int32, (1, width), 1) + at * width
        column = jnp.where(place < live, cell // ny, -1)
        hot_x = lax.broadcasted_iota(jnp.int32, (nx, width), 0) == column
        hot_y = lax.broadcasted_iota(jnp.int32, (ny, width), 0) == cell % ny
        total += lax.dot_general(
            hot_x.astype(jnp.float32).astype(jnp.bfloat16),
            hot_y.astype(jnp.float32).astype(jnp.bfloat16),
            NT,
            preferred_element_type=jnp.float32,
        )
    lon_m = 0.5 * lon_ref[...] * total
    lat_m = 0.5 * lat_ref[...] * total
    group = lon_t.shape[2]
    for at in range(nx // group):
        lon_t[at] = lon_m[at * group : (at + 1) * group].T
        lat_t[at] = lat_m[at * group : (at + 1) * group].T
    pl.semaphore_wait(barrier, jnp.where(lat > 0, 27, 26))

    def copy(src, dst, c, out, into, to):
        return pltpu.make_async_remote_copy(
            src_ref=src,
            dst_ref=dst,
            send_sem=send.at[c, out],
            recv_sem=recv.at[c, into],
            device_id=to,
            device_id_type=MESH,
        )

    def lanes(c):
        return pl.ds(pl.multiple_of(c * lane, lane), lane)

    def to_right(c):
        return copy(vt.at[nx, :, lanes(c)], vt.at[0, :, lanes(c)], c, 0, 0, right)

    def to_left(c):
        return copy(vt.at[1, :, lanes(c)], vt.at[nx + 1, :, lanes(c)], c, 1, 1, left)

    def to_up(c):
        return copy(edge16.at[1, c], from16.at[0, c], c, 2, 2, up)

    def to_fold(c):
        return copy(edge16.at[1, c], from16.at[1, c], c, 2, 3, up)

    def to_down(c):
        return copy(edge16.at[0, c], from16.at[1, c], c, 3, 3, down)

    def turn(step, _):
        c = lax.rem(step, 2) * 2 + step // 2
        load(step).wait()

        @pl.when(step < 3)
        def _():
            load(step + 1).start()

        wide[...] = vin[lax.rem(step, 2)].astype(jnp.float32)
        for x in range(nx):
            turned = wide[:, x, :].T
            vt[x + 1, :, lanes(c)] = turned.astype(jnp.bfloat16)
            edge[0, x : x + 1, :] = turned[:1, :]
            edge[1, x : x + 1, :] = turned[-1:, :]
        edge16[0, c] = edge[0].astype(jnp.bfloat16)
        edge16[1, c] = edge[1].astype(jnp.bfloat16)

        @pl.when(is_top)
        def _():
            to_fold(c).start()

        @pl.when(jnp.logical_not(is_top))
        def _():
            to_up(c).start()

        @pl.when(lat > 0)
        def _():
            to_down(c).start()

        to_right(c).start()
        to_left(c).start()
        return 0

    lax.fori_loop(0, 4, turn, 0)

    row = lax.broadcasted_iota(jnp.int32, (ny, 1), 0)
    iy = lax.broadcasted_iota(jnp.int32, (ny, ny), 0)
    ix = lax.broadcasted_iota(jnp.int32, (ny, ny), 1)
    band = (ix == iy + 1).astype(jnp.float32) - (ix == iy - 1).astype(jnp.float32)
    band = band.astype(jnp.bfloat16)
    acc[...] = jnp.zeros_like(acc)

    for h in range(2):
        for c in (h, 2 + h):
            to_right(c).wait_recv()
            to_left(c).wait_recv()
            to_fold(c).wait_recv()
            arrived = from16[1, c].astype(jnp.float32)
            north[c] = jnp.where(is_top, -arrived, arrived)

            @pl.when(lat == 0)
            def _():
                south[c] = jnp.zeros((nx, lane), jnp.float32)

            @pl.when(lat > 0)
            def _():
                to_up(c).wait_recv()
                south[c] = from16[0, c].astype(jnp.float32)

        cu, cv = h, 2 + h
        lu, lv = slice(cu * lane, cu * lane + lane), slice(cv * lane, cv * lane + lane)

        def fields(at_group, at, m_lon, m_lat):
            x = at_group * group + at
            x_top = x + top * (nx - 1 - 2 * x)
            here = pl.ds(x * ny if h else pl.multiple_of(x * ny, ny), ny)
            a, b = m_lon[:, at : at + 1], m_lat[:, at : at + 1]
            u_x = vt[x + 2, :, lu].astype(jnp.float32) - vt[x, :, lu].astype(jnp.float32)
            v_x = vt[x + 2, :, lv].astype(jnp.float32) - vt[x, :, lv].astype(jnp.float32)

            def over_y(c, where):
                inner = lax.dot_general(
                    band, vt[x + 1, :, where], NN, preferred_element_type=jnp.float32
                )
                inner = inner + jnp.where(row == ny - 1, north[c, pl.ds(x_top, 1), :], 0.0)
                return inner - jnp.where(row == 0, south[c, pl.ds(x, 1), :], 0.0)

            f[here, lu] = (a * v_x - b * over_y(cu, lu)).astype(jnp.bfloat16)
            f[here, lv] = (a * u_x + b * over_y(cv, lv)).astype(jnp.bfloat16)

        def multiply(at_group, low, high):
            span = pl.ds(at_group * group * ny, group * ny)
            acc[low:high, low:] += lax.dot_general(
                f[span, low:high], f[span, low:], TN, preferred_element_type=jnp.float32
            )

        def fields_of_group(at_group, _):
            m_lon, m_lat = lon_t[at_group], lat_t[at_group]
            for at in range(group):
                fields(at_group, at, m_lon, m_lat)
            return 0

        groups = nx // group
        middle = acc.shape[0] // 2
        if h == 0:
            lax.fori_loop(0, groups, fields_of_group, 0)
        else:
            for at_group in range(groups):
                m_lon, m_lat = lon_t[at_group], lat_t[at_group]
                for at in range(group):
                    fields(at_group, at, m_lon, m_lat)
                    if at_group and at == 3:
                        multiply(at_group - 1, 0, middle)
                    if at_group and at == 11:
                        multiply(at_group - 1, middle, 2 * middle)
            multiply(groups - 1, 0, middle)
            multiply(groups - 1, middle, 2 * middle)

    tile = 0
    for i in range(4):
        for j in range(i, 4):
            for k in range(16):
                half, spot, low = tile // 80, tile % 80 // 5, tile % 5 * 8
                g[half, spot, low : low + 8, :] = acc[
                    i * 128 + k * 8 : i * 128 + k * 8 + 8, j * 128 : (j + 1) * 128
                ]
                tile += 1
    cells, cols = f.shape
    spans = (pl.ds(0, 16), pl.ds(16, 16), pl.ds(32, 8))
    started = []

    def widen(at, _):
        here = pl.ds(pl.multiple_of(at * 128, 128), 128)
        spread[here] = f[here, :].astype(jnp.float32).reshape(128, 4, cols // 4)
        return 0

    def pick(at, _):
        base = at * 64
        taken = [spread[order[base + u]] for u in range(64)]
        for u in range(64):
            picked[base + u] = taken[u]
        return 0

    def pick_part(low, high):
        lax.fori_loop(low * 8, high * 8, pick, 0)

    def narrow(at, _):
        here = pl.ds(pl.multiple_of(at * 128, 128), 128)
        f[here, :] = picked[here].reshape(128, cols).astype(jnp.bfloat16)
        return 0

    def go(src, dst, out_sem, in_sem, to):
        item = pltpu.make_async_remote_copy(
            src_ref=src,
            dst_ref=dst,
            send_sem=out_sem,
            recv_sem=in_sem,
            device_id=to,
            device_id_type=MESH,
        )
        item.start()
        started.append(item)
        return item

    def pair_start(k):
        span = spans[k]
        return go(g.at[1 - core, :, span], r0.at[:, span], send0.at[k], recv0.at[k], mate)

    def gather_start(k, item):
        span = spans[k]
        item.wait_recv()
        s0[:, span] = g[core, :, span] + r0[:, span]
        items = []
        for off in range(1, 16):
            spot, to = plane(off)
            items.append(
                go(
                    s0.at[spot, span],
                    r1.at[mine, span],
                    send1.at[k, off - 1],
                    recv1.at[k, off - 1],
                    to,
                )
            )
        r1[mine, span] = s0[mine, span]
        return items

    def column_start(k, items):
        span = spans[k]
        for item in items:
            item.wait_recv()
        total = r1[0, span]
        for at in range(1, 16):
            total = total + r1[at, span]
        s1[0, span] = total
        r2[cz, span] = total
        return [
            go(
                s1.at[0, span],
                r2.at[cz, span],
                send2.at[k, off - 1],
                recv2.at[k, off - 1],
                along_z(off),
            )
            for off in range(1, 8)
        ]

    def back_start(k, items):
        span = spans[k]
        for item in items:
            item.wait_recv()
        total = r2[0, span]
        for at in range(1, 8):
            total = total + r2[at, span]
        s1[1, span] = total
        r3[mine, span] = total
        return [
            go(
                s1.at[1, span],
                r3.at[mine, span],
                send3.at[k, off - 1],
                recv3.at[k, off - 1],
                plane(off)[1],
            )
            for off in range(1, 16)
        ]

    def last_start(k, items):
        span = spans[k]
        for item in items:
            item.wait_recv()
        return go(r3.at[:, span], out.at[core, :, span], send4.at[k], recv4.at[k], mate)

    parts = range(len(spans))
    pairs = [pair_start(k) for k in parts]
    lax.fori_loop(0, cells // 128, widen, 0)
    planes = [gather_start(k, pairs[k]) for k in parts]
    pick_part(0, 3)
    columns = []
    for k in parts:
        columns.append(column_start(k, planes[k]))
        pick_part(3 + k, 4 + k)
    pick_part(6, 7)
    backs = []
    for k in parts:
        backs.append(back_start(k, columns[k]))
        pick_part(7 + k, 8 + k)
    pick_part(10, 12)
    lax.fori_loop(0, cells // 128, narrow, 0)
    store = pltpu.make_async_copy(f, t_hbm, store_sem)
    store.start()
    lasts = [last_start(k, backs[k]) for k in parts]
    out[core] = r3[...]
    for item in lasts:
        item.wait_recv()
    store.wait()
    for item in started:
        item.wait_send()
    for c in range(4):
        to_right(c).wait_send()
        to_left(c).wait_send()

        @pl.when(is_top)
        def _():
            to_fold(c).wait_send()

        @pl.when(jnp.logical_not(is_top))
        def _():
            to_up(c).wait_send()

        @pl.when(lat > 0)
        def _():
            to_down(c).wait_send()


def exact(a, b, dims):
    return lax.dot_general(
        a, b, dims, precision=lax.Precision.HIGHEST, preferred_element_type=jnp.float32
    )


def tree(terms):
    while len(terms) > 1:
        odd = terms[-1:] if len(terms) % 2 else []
        terms = [p + q for p, q in zip(terms[0::2], terms[1::2])] + odd
    return terms[0]


def eliminate(a, beside):
    n = a.shape[0]
    b = 8
    rows = [a[b * i : b * i + b, :] for i in range(n // b)]
    ci = lax.broadcasted_iota(jnp.int32, (b, n), 1)
    ri = lax.broadcasted_iota(jnp.int32, (b, n), 0)
    unit = [jnp.where(ri == j, 1.0, 0.0) for j in range(b)]

    def lane(v, c):
        return jnp.broadcast_to(v[:, c : c + 1], (b, n))

    pivot = [lane(rows[0], j) for j in range(b)]
    uppers, inverses = [], []
    for p in range(n // b):
        q = rows[p]
        x = list(unit)
        inside = (ci >= b * p) & (ci < b * p + b)
        q1 = jnp.where(inside, jnp.where(ci - b * p == ri, 1.0, 0.0), q)
        more = p + 1 < n // b
        if more:
            below = rows[p + 1]
            below_old = [lane(below, b * p + j) for j in range(b)]
            below_new = [lane(below, b * p + b + j) for j in range(b)]
            ahead = [lane(q, b * p + b + j) for j in range(b)]
        for k in range(b):
            value = jnp.broadcast_to(pivot[k][k : k + 1, :], (b, n))
            inv = 1.0 / value
            root = lax.rsqrt(value)
            col = jnp.where(ri == k, 0.0, pivot[k])
            fac = jnp.where(ri == k, -1.0, pivot[k])
            col_inv = col * inv
            under = jnp.where(ri > k, col_inv, 0.0)
            fresh = []
            for j in range(b):
                if j == k:
                    fresh.append(jnp.where(ri == k, inv, -col_inv))
                else:
                    fresh.append(
                        jnp.where(ri == k, 0.0, pivot[j]) - (fac * pivot[j][k : k + 1, :]) * inv
                    )
            pivot = fresh
            gain = jnp.where(ri == k, root, 1.0)
            for j in range(k + 1):
                x[j] = (x[j] - under * x[j][k : k + 1, :]) * gain
        z = tree([pivot[j] * q1[j : j + 1, :] for j in range(b)])
        if more:
            pivot_next = []
            for c in range(b):
                part = tree([pivot[j] * ahead[c][j : j + 1, :] for j in range(b)])
                pivot_next.append(
                    below_new[c] - tree([below_old[k] * part[k : k + 1, :] for k in range(b)])
                )
        z_rows = [jnp.broadcast_to(z[j : j + 1, :], (b, n)) for j in range(b)]
        for i in range(p + 1, n // b):
            src = rows[i]
            rows[i] = jnp.where(inside, 0.0, src) - tree(
                [lane(src, b * p + j) * z_rows[j] for j in range(b)]
            )
        upper = tree([x[j] * q[j : j + 1, :] for j in range(b)])
        inverse = tree([x[j] * q1[j : j + 1, :] for j in range(b)])
        diag = ci - b * p >= ri
        uppers.append(jnp.where(diag, upper, 0.0))
        inverses.append(jnp.where(ci - b * p <= ri, inverse, 0.0))
        if more:
            pivot = pivot_next
        for _ in range(-(-len(beside) // (n // b - p))):
            beside.pop(0)()
    return jnp.concatenate(uppers, axis=0), jnp.concatenate(inverses, axis=0)


def factor_kernel(scale, g_ref, t_hbm, o_hbm, r_ref, rows, w_ref, stage, in_sem, out_sem):
    load = pltpu.make_async_copy(t_hbm, rows, in_sem)
    load.start()
    b, n = 128, 4
    chunk = PIECE
    pieces = rows.shape[0] // chunk
    g, r, w, held, outs = {}, {}, {}, {}, []
    at = 0
    for i in range(n):
        for j in range(i, n):
            g[i, j] = g_ref[at]
            at += 1

    def spot(i, j):
        return slice(i * b, (i + 1) * b), slice(j * b, (j + 1) * b)

    def row_of(p, j):
        r[p, j] = exact(w[p, p], g[p, j], NN)

    def update(p, i, j):
        g[i, j] = g[i, j] - exact(r[p, i], r[p, j], TN)

    def hold(i, j):
        held[i, j] = tree([exact(r[k, i], w[k, j], TN) for k in range(j, i)])

    def store_w(i, j):
        value = w[i, j] * scale
        high = value.astype(jnp.bfloat16)
        low = (value - high.astype(jnp.float32)).astype(jnp.bfloat16)
        w_ref[2 * i * b : (2 * i + 1) * b, spot(i, j)[1]] = high
        w_ref[(2 * i + 1) * b : (2 * i + 2) * b, spot(i, j)[1]] = low

    def finish_row(p):
        if p:
            behind = exact(w[p, p], jnp.concatenate([held[p, j] for j in range(p)], axis=1), NN)
            for j in range(p):
                w[p, j] = -behind[:, j * b : (j + 1) * b]
        for j in range(p + 1):
            store_w(p, j)

    def store_r(p):
        for j in range(n):
            r_ref[spot(p, j)] = r[p, j] * (1.0 / scale) if j >= p else jnp.zeros((b, b), jnp.float32)

    def basis_piece(p, at):
        end = (p + 1) * b
        here = slice(at * chunk, (at + 1) * chunk)
        both = lax.dot_general(
            w_ref[2 * p * b : (2 * p + 2) * b, :end],
            rows[here, :end],
            NT,
            preferred_element_type=jnp.float32,
        )
        stage[p, :, here] = (both[:b] + both[b:]).astype(jnp.bfloat16)

    def send_row(p):
        item = pltpu.make_async_copy(stage.at[p], o_hbm.at[pl.ds(p * b, b), :], out_sem.at[p])
        item.start()
        outs.append(item)

    beside = []
    for p in range(n):
        r[p, p], w[p, p] = eliminate(g[p, p], beside)
        assert not beside
        if p == 0:
            load.wait()
        else:
            send_row(p - 1)
        if p + 1 < n:
            row_of(p, p + 1)
            update(p, p + 1, p + 1)
            for j in range(p + 2, n):
                beside.append(functools.partial(row_of, p, j))
                for i in range(p + 1, j + 1):
                    beside.append(functools.partial(update, p, i, j))
            beside.append(functools.partial(finish_row, p))
            for j in range(p + 1):
                beside.append(functools.partial(hold, p + 1, j))
            beside.append(functools.partial(store_r, p))
            for at in range(pieces):
                beside.append(functools.partial(basis_piece, p, at))
        else:
            finish_row(p)
            store_r(p)
            for at in range(pieces):
                basis_piece(p, at)
            send_row(p)
    for item in outs:
        item.wait()


def shards(n_lat, n_lon, velocity, lon_metric, lat_metric, wet_index, wet_count):
    days, nx, ny = velocity.shape[1:]
    cols = 2 * days
    cells = nx * ny
    f32, bf16 = jnp.float32, jnp.bfloat16
    shape = jax.ShapeDtypeStruct
    params = pltpu.CompilerParams(vmem_limit_bytes=BIG)

    dma = pltpu.SemaphoreType.DMA
    lane, group = 128, 16
    total, picked = pl.pallas_call(
        functools.partial(field_kernel, n_lat, n_lon),
        in_specs=[SMEM, VMEM, SMEM, VMEM, VMEM, ANY],
        out_specs=[VMEM, ANY],
        out_shape=[shape((2, 16, 40, 128), f32), shape((cells, cols), bf16)],
        scratch_shapes=[
            pltpu.VMEM((2, lane, nx, ny), bf16),
            pltpu.VMEM((lane, nx, ny), f32),
            pltpu.VMEM((nx + 2, ny, cols), bf16),
            pltpu.VMEM((cells, cols), bf16),
            pltpu.VMEM((nx // group, ny, group), f32),
            pltpu.VMEM((nx // group, ny, group), f32),
            pltpu.VMEM((cols, cols), f32),
            pltpu.VMEM((2, nx, lane), f32),
            pltpu.VMEM((2, 4, nx, lane), bf16),
            pltpu.VMEM((2, 4, nx, lane), bf16),
            pltpu.VMEM((4, nx, lane), f32),
            pltpu.VMEM((4, nx, lane), f32),
            pltpu.VMEM((cells, 4, cols // 4), f32),
            pltpu.VMEM((cells, 4, cols // 4), f32),
            pltpu.VMEM((2, 16, 40, 128), f32),
            pltpu.VMEM((16, 40, 128), f32),
            pltpu.VMEM((16, 40, 128), f32),
            pltpu.VMEM((16, 40, 128), f32),
            pltpu.VMEM((8, 40, 128), f32),
            pltpu.VMEM((2, 40, 128), f32),
            pltpu.VMEM((16, 40, 128), f32),
            dma((2,)),
            dma(()),
            dma((4, 4)),
            dma((4, 4)),
            *[dma((3,) + n) for n in ((), (), (15,), (15,), (7,), (7,), (15,), (15,), (), ())],
        ],
        compiler_params=pltpu.CompilerParams(
            collective_id=0, has_side_effects=True, vmem_limit_bytes=BIG
        ),
    )(
        wet_index,
        wet_index.reshape(nx, ny),
        wet_count,
        lon_metric,
        lat_metric,
        velocity.reshape(cols, nx, ny),
    )

    scale = math.sqrt(cells * n_lat * n_lon)
    basis, r_factor = pl.pallas_call(
        functools.partial(factor_kernel, scale),
        in_specs=[VMEM, ANY],
        out_specs=[ANY, VMEM],
        out_shape=[shape((cols, cells), bf16), shape((cols, cols), f32)],
        scratch_shapes=[
            pltpu.VMEM((cells, cols), bf16),
            pltpu.VMEM((2 * cols, cols), bf16),
            pltpu.VMEM((4, 128, cells), bf16),
            dma(()),
            dma((4,)),
        ],
        compiler_params=params,
    )(total.reshape(10, 128, 128), picked)
    return basis, r_factor


def solution(mesh):
    n_lat, n_lon = mesh.shape["lat"], mesh.shape["lon"]
    placed = (
        P(None, None, "lon", "lat"),
        P("lon", "lat"),
        P("lon", "lat"),
        P(("lat", "lon")),
        P(("lat", "lon")),
    )
    return jax.shard_map(
        functools.partial(shards, n_lat, n_lon),
        mesh=mesh,
        in_specs=placed,
        out_specs=(P(None, ("lat", "lon")), P()),
        check_vma=False,
    )
```
